32 devices in a mesh: layer: 2 (over core), latent: 16 (over z, y, x).
Axes of the slice: x: 2, y: 2, z: 4, core: 2. Of those that a mesh axis runs over, the one named last changes fastest.
Arguments:
- activations: bfloat16 [2, 512, 2048], P('layer', 'latent'), may hold values from -15 to 15
- enc_weight: bfloat16 [2, 2048, 16384], P('layer', None, 'latent'), may hold values from -0.09375 to 0.09375
- enc_bias: float32 [16384], P('latent'), may hold values from -3 to 3
- dec_weight: bfloat16 [2, 16384, 2048], P('layer', 'latent'), may hold values from -0.1796875 to 0.1796875
- dec_bias: float32 [2, 2048], P('layer'), may hold values from -3 to 3
- active_mask: int32 [512, 16384], P(None, 'latent'), may hold values 0 or 1
Outputs:
- grad_enc: bfloat16 [2, 2048, 16384], P('layer', None, 'latent')
- grad_dec: bfloat16 [2, 16384, 2048], P('layer', 'latent')
- loss_value: float32 [], replicated
The draws below stay inside these ranges and needn't reach their ends.
All inputs are finite; a program needn't handle non-finite values. No bound on the sum of `active_mask` on one device may be relied on, other than what follows from the above.
Results may differ from the reference program's by a relative error of at most 0.0065.
Values may be sent and summed in bfloat16 or wider, within the bound.
A program may use at most 128 MiB of HBM per device.

```python
import jax
import jax.numpy as jnp
from jax import lax

D = 2048
TOK = 512
LAYERS = 2
LATENTS = 16384


def draw_activations(key, part):
    first = jax.random.fold_in(key, 0)
    layer_scale = 1.0 + 0.8 * jnp.arange(LAYERS, dtype=jnp.float32)[:, None, None] / max(LAYERS - 1, 1)
    base = jnp.clip(jax.random.normal(first, (LAYERS, TOK, D), jnp.float32), -7.0, 7.0)
    values = base * layer_scale
    return values.astype(jnp.bfloat16)


def draw_dec_weight(key, part):
    first = jax.random.fold_in(key, 0)
    rising = 3.0 ** (jnp.arange(LATENTS, dtype=jnp.float32) / LATENTS)
    layer_scale = 1.0 + 0.8 * jnp.arange(LAYERS, dtype=jnp.float32)[:, None, None] / max(LAYERS - 1, 1)
    factor = (2.0 * LATENTS) ** (-0.5)
    base = jnp.clip(jax.random.normal(first, (LAYERS, LATENTS, D), jnp.float32), -6.0, 6.0)
    values = base * rising[None, :, None] * layer_scale * factor
    return values.astype(jnp.bfloat16)


def touch_ends(array, stream_key, smallest, top_value):
    dims = array.shape
    place = [jax.random.randint(jax.random.fold_in(stream_key, axis), (), 0, dims[axis]) for axis in range(len(dims))]
    array = array.at[tuple(place)].set(smallest)
    longest = dims.index(max(dims))
    place[longest] = (place[longest] + 1) % dims[longest]
    return array.at[tuple(place)].set(top_value)


def block_scale(key, dims, shards, least, largest):
    factor_of = 1.0
    for position, blocks in shards:
        heights = jax.random.uniform(jax.random.fold_in(jax.random.fold_in(key, 6), position), (blocks,), jnp.float32, least / len(shards), largest / len(shards))
        factor_of = factor_of * jnp.repeat(jnp.exp(heights), dims[position] // blocks).reshape((-1,) + (1,) * (len(dims) - 1 - position))
    return factor_of


def scatter_about(rng, shape, width, limit, cuts=(), kind=jnp.bfloat16):
    drawn = jax.random.normal(rng, shape, jnp.float32) * width
    if len(cuts) > 0:
        drawn = block_scale(rng, shape, cuts, -0.22, 0.18) * drawn
    return jnp.clip(drawn, min=-limit, max=limit).astype(kind)


def setup_inputs(seed: int = 0) -> dict:
    streams_of = jax.random.split(jax.random.key(seed), 7)
    return {
        "activations": draw_activations(jax.random.fold_in(streams_of[6], 71), 0),
        "enc_weight": scatter_about(streams_of[1], (LAYERS, D, LATENTS), (LAYERS * D) ** -0.5, 0.09375, ((0, 2), (2, 16))),
        "enc_bias": scatter_about(streams_of[2], (LATENTS,), 0.5, 3.0, ((0, 16),), jnp.float32),
        "dec_weight": draw_dec_weight(jax.random.fold_in(streams_of[6], 71), 0),
        "dec_bias": scatter_about(streams_of[4], (LAYERS, D), 0.5, 3.0, ((0, 2),), jnp.float32),
        "active_mask": touch_ends((jax.random.randint(streams_of[5], (TOK, LATENTS), 0, 4) < 1).astype(jnp.int32), jax.random.fold_in(streams_of[5], 1), 0, 1),
    }


sparsity_weight = 0.4

def reference(activations, enc_weight, enc_bias, dec_weight, dec_bias, active_mask):
    preact = jnp.zeros((TOK, LATENTS), jnp.float32)
    for layer in range(LAYERS):
        preact = preact + jnp.dot(activations[layer], enc_weight[layer], preferred_element_type=jnp.float32)
    preact = preact + enc_bias
    gating = active_mask.astype(jnp.float32)
    latent_code = preact * gating
    code_b = latent_code.astype(jnp.bfloat16)
    norm_list = []
    for layer in range(LAYERS):
        dec_float = dec_weight[layer].astype(jnp.float32)
        norm_list.append(jnp.sqrt(lax.optimization_barrier(jnp.sum(dec_float * dec_float, axis=1)) + 1e-06))
    norm_sum = norm_list[0]
    for layer in range(1, LAYERS):
        norm_sum = norm_sum + norm_list[layer]
    square_part = jnp.float32(0.0)
    error_list = []
    code_grad = jnp.zeros((TOK, LATENTS), jnp.float32)
    for layer in range(LAYERS):
        recon = jnp.dot(code_b, dec_weight[layer], preferred_element_type=jnp.float32) + dec_bias[layer]
        error_full = recon - activations[layer].astype(jnp.float32)
        square_part = square_part + 0.5 * jnp.sum(error_full * error_full)
        error_b = error_full.astype(jnp.bfloat16)
        error_list.append(error_b)
        code_grad = code_grad + jnp.dot(error_b, dec_weight[layer].T, preferred_element_type=jnp.float32)
    code_grad = code_grad + sparsity_weight * norm_sum
    preact_grad = (code_grad * gating).astype(jnp.bfloat16)
    code_total = lax.optimization_barrier(jnp.sum(latent_code, axis=0))
    enc_list = []
    dec_list = []
    for layer in range(LAYERS):
        enc_list.append(jnp.dot(activations[layer].T, preact_grad, preferred_element_type=jnp.float32).astype(jnp.bfloat16))
        dec_float = dec_weight[layer].astype(jnp.float32)
        shrink = sparsity_weight * code_total[:, None] * dec_float / norm_list[layer][:, None]
        dec_list.append((jnp.dot(code_b.T, error_list[layer], preferred_element_type=jnp.float32) + shrink).astype(jnp.bfloat16))
    sparse_part = sparsity_weight * jnp.sum(latent_code * norm_sum)
    loss_value = (square_part + sparse_part) / (TOK * D)
    return (jnp.stack(enc_list), jnp.stack(dec_list), loss_value)
```

```python
import functools

import jax
import jax.numpy as jnp
from jax import lax
from jax.experimental import pallas as pl
from jax.experimental.pallas import tpu as pltpu
from jax.sharding import PartitionSpec as P

sparsity_weight = 0.4
MESH = pl.DeviceIdType.MESH
F32 = jnp.float32
BF16 = jnp.bfloat16


def plain_step(activations, enc_weight, enc_bias, dec_weight, dec_bias, active_mask):
    local_rows = activations[0]
    encoder = enc_weight[0]
    decoder = dec_weight[0]
    token_all = lax.all_gather(local_rows, "latent", axis=0, tiled=True)
    layer_pre = jnp.dot(token_all, encoder, preferred_element_type=jnp.float32)
    dec_float = decoder.astype(jnp.float32)
    row_norm = jnp.sqrt(jnp.sum(dec_float * dec_float, axis=1) + 1e-06)
    preact, norm_sum = lax.psum((layer_pre, row_norm), "layer")
    preact = preact + enc_bias
    gating = active_mask.astype(jnp.float32)
    latent_code = preact * gating
    code_b = latent_code.astype(jnp.bfloat16)
    layer_index = lax.axis_index("layer")
    recon_share = (
        lax.psum_scatter(
            jnp.dot(code_b, decoder, preferred_element_type=jnp.float32),
            "latent",
            scatter_dimension=0,
            tiled=True,
        )
        + dec_bias[0]
    )
    error_share = recon_share - local_rows.astype(jnp.float32)
    square_part = 0.5 * jnp.sum(error_share * error_share)
    error_b = lax.all_gather(error_share.astype(jnp.bfloat16), "latent", axis=0, tiled=True)
    layer_grad = jnp.einsum("td,fd->tf", error_b, decoder, preferred_element_type=jnp.float32)
    code_grad = lax.psum(layer_grad, "layer") + sparsity_weight * norm_sum
    preact_grad = (code_grad * gating).astype(jnp.bfloat16)
    grad_enc = jnp.einsum(
        "td,tf->df", token_all, preact_grad, preferred_element_type=jnp.float32
    ).astype(jnp.bfloat16)
    code_total = jnp.sum(latent_code, axis=0)
    shrink = sparsity_weight * code_total[:, None] * dec_float / row_norm[:, None]
    grad_dec = (
        jnp.einsum("tf,td->fd", code_b, error_b, preferred_element_type=jnp.float32) + shrink
    ).astype(jnp.bfloat16)
    sparse_part = jnp.where(
        layer_index == 0, sparsity_weight * jnp.sum(latent_code * norm_sum), 0.0
    )
    loss_total = lax.psum(square_part + sparse_part, ("layer", "latent"))
    loss_value = loss_total / (active_mask.shape[0] * token_all.shape[1])
    return (grad_enc[None], grad_dec[None], loss_value)


def exchange_kernel(n, group, act, enc_hbm, bias, dec_hbm, dbias, mask_hbm,
                    tok_t_out, code_t_out, err_out, pg_out, coef, loss_out,
                    enc, dec, mask, tok, tok_t, pre_own, pre_recv, code, code_t,
                    rs_send, rs_recv, rs_half, up_send, up_recv, err, lg_own, lg_recv, pg,
                    norm_own, norm_recv, total, loss_send, loss_recv, pair_send, pair_recv,
                    load_sem, out_sem, ag_z, ag_s, ag_r, ag_h, ag_hr, rs_s, rs_r, rs_h, rs_hr,
                    up_s, up_r, er_z, er_s, er_r, er_h, er_hr, ls_s, ls_r,
                    pre_s, pre_r, lg_s, lg_r, nm_s, nm_r, pl_s, pl_r):
    me = lax.axis_index("latent")
    layer = lax.axis_index("layer")
    other = 1 - layer
    rows, width = act.shape
    tokens, latents = mask.shape
    span = group * rows
    groups = n // group
    mine = me // group
    spot = lax.rem(me, group)
    edge = jnp.minimum(mine, groups - 1 - mine)
    low_side = mine <= groups - 1 - mine

    def place(step):
        half = (step + 1) // 2
        near = mine + jnp.where(lax.rem(step, 2) == 1, half, -half)
        rest = jnp.where(low_side, step, groups - 1 - step)
        return jnp.where(step <= 2 * edge, near, rest)

    side_x = spot ^ 1
    side_y = spot ^ 2
    corner = spot ^ 3
    half_rows = rows // 2

    def half(k):
        return pl.ds(k * half_rows, half_rows)

    loads = [
        pltpu.make_async_copy(hbm, vmem, load_sem.at[i])
        for i, (hbm, vmem) in enumerate(((dec_hbm, dec), (enc_hbm, enc), (mask_hbm, mask)))
    ]
    for load in loads:
        load.start()

    barrier = pltpu.get_barrier_semaphore()

    def greet(index, carry):
        pl.semaphore_signal(barrier, inc=1, device_id={"latent": lax.rem(me + index, n)}, device_id_type=MESH)
        return carry

    lax.fori_loop(1, n, greet, 0)
    pl.semaphore_signal(barrier, inc=1, device_id={"layer": other}, device_id_type=MESH)
    pl.semaphore_wait(barrier, n)

    def latent_copy(src, dst, send, recv, target):
        return pltpu.make_async_remote_copy(
            src_ref=src, dst_ref=dst, send_sem=send, recv_sem=recv,
            device_id={"latent": target}, device_id_type=MESH)

    def layer_copy(src, dst, send, recv):
        return pltpu.make_async_remote_copy(
            src_ref=src, dst_ref=dst, send_sem=send, recv_sem=recv,
            device_id={"layer": other}, device_id_type=MESH)

    def loop(lower, upper, do):
        def body(index, carry):
            do(index)
            return carry
        lax.fori_loop(lower, upper, body, 0)

    def each_peer(do):
        loop(1, n, lambda index: do(lax.rem(me + index, n)))

    class Gather:
        def __init__(self, buf, first, z_sem, send_sem, recv_sem, half_sem, half_recv):
            self.buf, self.first = buf, first
            self.z_sem, self.send_sem, self.recv_sem = z_sem, send_sem, recv_sem
            self.half_sem, self.half_recv = half_sem, half_recv

        def own(self, shift):
            return latent_copy(
                self.first, self.buf.at[me], self.z_sem.at[mine if shift > 0 else groups],
                self.recv_sem.at[me], me + shift * group)

        def each_own(self, do):
            @pl.when(mine < groups - 1)
            def _():
                do(self.own(1))

            @pl.when(mine > 0)
            def _():
                do(self.own(-1))

        def onward(self, step, do):
            g = place(step)
            to = mine + jnp.where(g < mine, 1, -1)
            block = g * group + spot

            @pl.when((to >= 0) & (to < groups))
            def _():
                do(latent_copy(
                    self.buf.at[block], self.buf.at[block], self.z_sem.at[g],
                    self.recv_sem.at[block], to * group + spot))

        def sides(self, step, do, own=False):
            g = place(step)
            block = g * group + spot
            for i, to in enumerate((side_x, side_y)):
                do(latent_copy(
                    self.first if own else self.buf.at[block], self.buf.at[block],
                    self.send_sem.at[i, g], self.recv_sem.at[block], mine * group + to))

        def turn(self, step, k):
            g = place(step)
            source, to = ((side_x, side_y), (side_y, side_x))[k]
            part = self.buf.at[g * group + source, half(k)]
            return latent_copy(
                part, part, self.half_sem.at[k, g], self.half_recv.at[k, g], mine * group + to)

        def arrived(self, block):
            latent_copy(
                self.buf.at[block], self.buf.at[block],
                self.z_sem.at[0], self.recv_sem.at[block], me).wait_recv()

        def start(self):
            self.sides(0, lambda copy: copy.start(), own=True)
            self.each_own(lambda copy: copy.start())

        def chain(self, step):
            self.arrived(place(step) * group + spot)
            self.onward(step, lambda copy: copy.start())
            self.sides(step, lambda copy: copy.start())

        def relay(self, step):
            g = place(step)
            for k, source in enumerate((side_x, side_y)):
                self.arrived(g * group + source)
                self.turn(step, k).start()

        def wait_corner(self, step):
            g = place(step)
            for k in range(2):
                part = self.buf.at[g * group + corner, half(k)]
                latent_copy(
                    part, part, self.half_sem.at[k, g], self.half_recv.at[k, g], me).wait_recv()

        def finish(self):
            self.each_own(lambda copy: copy.wait_send())
            self.sides(0, lambda copy: copy.wait_send(), own=True)

            def done(k):
                self.onward(k, lambda copy: copy.wait_send())
                self.sides(k, lambda copy: copy.wait_send())

            loop(1, groups, done)
            loop(0, groups, lambda k: [self.turn(k, h).wait_send() for h in range(2)] and None)

    tokens_in = Gather(tok, act, ag_z, ag_s, ag_r, ag_h, ag_hr)
    tokens_in.start()
    tok[me] = act[...]

    loads[0].wait()
    lanes = 128

    def norm_block(block, carry):
        at = pl.multiple_of(block * lanes, lanes)
        piece = dec[pl.ds(at, lanes), :].astype(F32)
        sums = jnp.sum(piece * piece, axis=1, keepdims=True)
        norm = jnp.sqrt(sums + 1e-06)
        norm_own[:, pl.ds(at, lanes)] = jnp.broadcast_to(norm, (lanes, lanes)).T[0:8, :]
        return carry

    lax.fori_loop(0, latents // lanes, norm_block, 0)
    norm_copy = layer_copy(norm_own, norm_recv, nm_s, nm_r)
    norm_copy.start()
    total[...] = jnp.zeros_like(total)
    loads[1].wait()
    loads[2].wait()

    def rows_of(g):
        return pl.ds(pl.multiple_of(g * span, span), span)

    def pre_copy(g):
        return layer_copy(pre_own.at[g], pre_recv.at[g], pre_s.at[g], pre_r.at[g])

    def lg_copy(g):
        return layer_copy(lg_own.at[g], lg_recv.at[g], lg_s.at[g], lg_r.at[g])

    def corner_copy(g, k):
        return latent_copy(
            rs_send.at[g * group + corner, half(k)], rs_half.at[k, g],
            rs_h.at[k, g], rs_hr.at[k, g], mine * group + (side_y, side_x)[k])

    def side_copy(g, i, k):
        to = (side_x, side_y)[i]
        return latent_copy(
            rs_send.at[g * group + to, half(k)], rs_recv.at[g * group + spot, half(k)],
            rs_s.at[i, k, g], rs_r.at[g * group + spot], mine * group + to)

    def side_arrived(g):
        for source in (side_x, side_y):
            block = g * group + source
            latent_copy(
                rs_send.at[block], rs_recv.at[block], rs_s.at[0, 0, g], rs_r.at[block],
                me).wait_recv()

    def up_copy(g):
        return latent_copy(
            up_send.at[g], up_recv.at[mine], up_s.at[g], up_r.at[mine], g * group + spot)

    def up_arrived(g):
        latent_copy(up_send.at[g], up_recv.at[g], up_s.at[g], up_r.at[g], me).wait_recv()

    tile = min(512, latents)
    wide = min(512, width)

    def encode(step):
        g = place(step)
        tokens_in.wait_corner(step)
        left = tok[pl.ds(g * group, group)].reshape(span, width)
        for c in range(latents // tile):
            cols = pl.ds(c * tile, tile)
            part = jnp.dot(left, enc[:, cols], preferred_element_type=F32)
            pre_own[g, :, cols] = part
        pre_copy(g).start()
        tok_t[:, rows_of(g)] = left.T

    def decode(step):
        g = place(step)
        pre_copy(g).wait_recv()
        here = rows_of(g)
        for c in range(latents // tile):
            cols = pl.ds(c * tile, tile)
            preact = pre_own[g, :, cols] + pre_recv[g, :, cols] + bias[0:1, cols]
            latent = preact * mask[here, cols].astype(F32)
            total[0:1, cols] += jnp.sum(latent, axis=0, keepdims=True)
            code[here, cols] = latent.astype(BF16)
        code_t[:, here] = code[here, :].T

    def reconstruct(step):
        g = place(step)
        left = code[rows_of(g), :]
        for c in range(width // wide):
            cols = pl.ds(c * wide, wide)
            part = jnp.dot(left, dec[:, cols], preferred_element_type=F32).astype(BF16)
            rs_send[pl.ds(g * group, group), :, cols] = part.reshape(group, rows, wide)
        for k in range(2):
            corner_copy(g, k).start()
            side_copy(g, k, 1 - k).start()

    def fold(step):
        g = place(step)
        for k, to in enumerate((side_x, side_y)):
            latent_copy(
                rs_half.at[k, g], rs_half.at[k, g], rs_h.at[k, g], rs_hr.at[k, g],
                me).wait_recv()
            at = (g * group + to, half(k))
            rs_send[at] = (rs_send[at].astype(F32) + rs_half[k, g].astype(F32)).astype(BF16)
            side_copy(g, k, k).start()

    def plane_sum(g, cols):
        part = rs_send[g * group + spot, :, cols].astype(F32)
        for source in (side_x, side_y):
            part = part + rs_recv[g * group + source, :, cols].astype(F32)
        return part

    def climb(step):
        g = place(step)
        side_arrived(g)
        for c in range(width // wide):
            cols = pl.ds(c * wide, wide)
            up_send[g, :, cols] = plane_sum(g, cols).astype(BF16)
        up_copy(g).start()

    def guarded(low, step, high, do):
        @pl.when((step >= low) & (step < high))
        def _():
            do(step)

    def forward(step):
        guarded(1, step + 1, groups, tokens_in.chain)
        guarded(0, step, groups, tokens_in.relay)
        guarded(0, step - 1, groups, encode)
        guarded(0, step - 2, groups, decode)
        guarded(1, step - 2, groups, reconstruct)
        guarded(1, step - 3, groups, fold)
        guarded(1, step - 4, groups, climb)

    loop(0, groups + 2, forward)
    reconstruct(0)
    fold(groups - 1)
    climb(groups - 2)
    fold(0)
    climb(groups - 1)

    outs = [
        pltpu.make_async_copy(vmem, hbm, out_sem.at[i])
        for i, (vmem, hbm) in enumerate(
            ((tok_t, tok_t_out), (code_t, code_t_out), (err, err_out), (pg, pg_out)))
    ]
    outs[0].start()
    outs[1].start()

    norm_copy.wait()
    norm_sum = norm_own[0:1, :] + norm_recv[0:1, :]
    sparse = sparsity_weight * jnp.sum(total[0:1, :] * norm_sum)
    ratio = sparsity_weight * total[0:1, :] / norm_own[0:1, :]
    coef[...] = jnp.broadcast_to(ratio, (128, latents)).T
    norm_recv[...] = jnp.broadcast_to(sparsity_weight * norm_sum, norm_recv.shape)

    side_arrived(mine)
    loop(1, groups, lambda k: up_arrived(place(k)))
    squares = jnp.zeros((1, 1), F32)
    for c in range(width // wide):
        cols = pl.ds(c * wide, wide)
        recon = plane_sum(mine, cols)
        for j in range(1, groups):
            recon = recon + up_recv[lax.rem(mine + j, groups), :, cols].astype(F32)
        error = recon + dbias[0:1, cols] - act[:, cols].astype(F32)
        squares = squares + jnp.sum(error * error)
        err[me, :, cols] = error.astype(BF16)
    partial = 0.5 * squares + jnp.where(layer == 0, sparse, 0.0)
    loss_send[...] = jnp.broadcast_to(partial, loss_send.shape)
    loss_recv[me] = loss_send[...]

    def loss_copy(target):
        return latent_copy(loss_send, loss_recv.at[me], ls_s.at[target], ls_r.at[me], target)

    def loss_wait(source):
        return latent_copy(loss_send, loss_recv.at[source], ls_s.at[source], ls_r.at[source], source)

    errors_in = Gather(err, err.at[me], er_z, er_s, er_r, er_h, er_hr)
    errors_in.start()
    each_peer(lambda t: loss_copy(t).start())

    def grad(step):
        g = place(step)
        errors_in.wait_corner(step)
        left = err[pl.ds(g * group, group)].reshape(span, width)
        for c in range(latents // tile):
            part = lax.dot_general(
                left, dec[pl.ds(c * tile, tile), :], (((1,), (1,)), ((), ())),
                preferred_element_type=F32)
            cols = pl.ds(c * tile, tile)
            lg_own[g, :, cols] = part
        lg_copy(g).start()

    def gate(step):
        g = place(step)
        here = rows_of(g)
        lg_copy(g).wait_recv()
        for c in range(latents // tile):
            cols = pl.ds(c * tile, tile)
            code_grad = lg_own[g, :, cols] + lg_recv[g, :, cols] + norm_recv[0:1, cols]
            pg[here, cols] = (code_grad * mask[here, cols].astype(F32)).astype(BF16)

    def backward(step):
        guarded(1, step + 1, groups, errors_in.chain)
        guarded(0, step, groups, errors_in.relay)
        guarded(0, step - 1, groups, grad)
        guarded(0, step - 2, groups - 1, gate)

    loop(0, groups + 1, backward)
    outs[2].start()
    each_peer(lambda s: loss_wait(s).wait_recv())
    pair_send[...] = jnp.sum(loss_recv[...], axis=0)
    pair = layer_copy(pair_send, pair_recv, pl_s, pl_r)
    pair.start()
    gate(groups - 1)
    outs[3].start()

    tokens_in.finish()
    errors_in.finish()
    each_peer(lambda t: loss_copy(t).wait_send())
    loop(1, groups, lambda k: up_copy(place(k)).wait_send())

    def finish_group(g):
        pre_copy(g).wait_send()
        lg_copy(g).wait_send()
        for k in range(2):
            corner_copy(g, k).wait_send()
            for i in range(2):
                side_copy(g, i, k).wait_send()

    loop(0, groups, finish_group)
    pair.wait()
    loss_out[...] = (pair_send[...] + pair_recv[...]) / (tokens * width)
    for out in outs:
        out.wait()


def grads_kernel(tok_t, pg, code_t, err, dec, coef, loss, enc_out, dec_out, loss_out):
    loss_out[...] = loss[0:1, 0:1]
    enc_out[...] = jnp.dot(tok_t[...], pg[...], preferred_element_type=F32).astype(BF16)
    shrink = coef[:, 0:1] * dec[...].astype(F32)
    dec_out[...] = (jnp.dot(code_t[...], err[...], preferred_element_type=F32) + shrink).astype(BF16)


def fast_step(n, activations, enc_weight, enc_bias, dec_weight, dec_bias, active_mask):
    rows, width = activations.shape[1:]
    tokens, latents = active_mask.shape
    group = 4
    groups = n // group
    span = group * rows
    decoder = dec_weight[0]
    vmem = pl.BlockSpec(memory_space=pltpu.VMEM)
    anyw = pl.BlockSpec(memory_space=pl.ANY)
    hbm = pl.BlockSpec(memory_space=pltpu.HBM)
    shape = jax.ShapeDtypeStruct
    dma = pltpu.SemaphoreType.DMA
    tok_t, code_t, err, pg, coef, loss = pl.pallas_call(
        functools.partial(exchange_kernel, n, group),
        out_shape=(
            shape((width, tokens), BF16),
            shape((latents, tokens), BF16),
            shape((n, rows, width), BF16),
            shape((tokens, latents), BF16),
            shape((latents, 128), F32),
            shape((8, 128), F32),
        ),
        in_specs=[vmem, hbm, vmem, hbm, vmem, hbm],
        out_specs=(anyw, anyw, anyw, anyw, vmem, vmem),
        scratch_shapes=[
            pltpu.VMEM((width, latents), BF16),
            pltpu.VMEM((latents, width), BF16),
            pltpu.VMEM((tokens, latents), jnp.int32),
            pltpu.VMEM((n, rows, width), BF16),
            pltpu.VMEM((width, tokens), BF16),
            pltpu.VMEM((groups, span, latents), F32),
            pltpu.VMEM((groups, span, latents), F32),
            pltpu.VMEM((tokens, latents), BF16),
            pltpu.VMEM((latents, tokens), BF16),
            pltpu.VMEM((n, rows, width), BF16),
            pltpu.VMEM((n, rows, width), BF16),
            pltpu.VMEM((2, groups, rows // 2, width), BF16),
            pltpu.VMEM((groups, rows, width), BF16),
            pltpu.VMEM((groups, rows, width), BF16),
            pltpu.VMEM((n, rows, width), BF16),
            pltpu.VMEM((groups, span, latents), F32),
            pltpu.VMEM((groups, span, latents), F32),
            pltpu.VMEM((tokens, latents), BF16),
            pltpu.VMEM((8, latents), F32),
            pltpu.VMEM((8, latents), F32),
            pltpu.VMEM((8, latents), F32),
            pltpu.VMEM((8, 128), F32),
            pltpu.VMEM((n, 8, 128), F32),
            pltpu.VMEM((8, 128), F32),
            pltpu.VMEM((8, 128), F32),
            dma((3,)), dma((4,)),
            dma((groups + 1,)), dma((2, groups)), dma((n,)), dma((2, groups)), dma((2, groups)),
            dma((2, 2, groups)), dma((n,)), dma((2, groups)), dma((2, groups)),
            dma((groups,)), dma((groups,)),
            dma((groups + 1,)), dma((2, groups)), dma((n,)), dma((2, groups)), dma((2, groups)),
            dma((n,)), dma((n,)),
            dma((groups,)), dma((groups,)), dma((groups,)), dma((groups,)),
            dma, dma, dma, dma,
        ],
        compiler_params=pltpu.CompilerParams(
            collective_id=0, has_side_effects=True, vmem_limit_bytes=46 << 20),
    )(activations[0], enc_weight[0], enc_bias[None], decoder, dec_bias, active_mask)
    err = err.reshape(tokens, width)
    tile = min(512, latents)
    grad_enc, grad_dec, loss = pl.pallas_call(
        grads_kernel,
        grid=(latents // tile,),
        out_shape=(
            shape((width, latents), BF16),
            shape((latents, width), BF16),
            shape((1, 1), F32),
        ),
        in_specs=[
            pl.BlockSpec((width, tokens), lambda i: (0, 0)),
            pl.BlockSpec((tokens, tile), lambda i: (0, i)),
            pl.BlockSpec((tile, tokens), lambda i: (i, 0)),
            pl.BlockSpec((tokens, width), lambda i: (0, 0)),
            pl.BlockSpec((tile, width), lambda i: (i, 0)),
            pl.BlockSpec((tile, 128), lambda i: (i, 0)),
            pl.BlockSpec((8, 128), lambda i: (0, 0)),
        ],
        out_specs=(
            pl.BlockSpec((width, tile), lambda i: (0, i)),
            pl.BlockSpec((tile, width), lambda i: (i, 0)),
            pl.BlockSpec((1, 1), lambda i: (0, 0)),
        ),
        compiler_params=pltpu.CompilerParams(vmem_limit_bytes=24 << 20),
    )(tok_t, pg, code_t, err, decoder, coef, loss)
    return (grad_enc[None], grad_dec[None], loss.reshape(()))


def solution(mesh):
    placed = (
        P("layer", "latent", None),
        P("layer", None, "latent"),
        P("latent"),
        P("layer", "latent", None),
        P("layer", None),
        P(None, "latent"),
    )
    n = mesh.shape["latent"]

    def per_device(activations, *others):
        rows = activations.shape[1]
        if rows == 32 and n % 4 == 0:
            return fast_step(n, activations, *others)
        return plain_step(activations, *others)

    return jax.shard_map(
        per_device,
        mesh=mesh,
        in_specs=placed,
        out_specs=(P("layer", None, "latent"), P("layer", "latent", None), P()),
        check_vma=False,
    )
```

```python
import functools

import jax
import jax.numpy as jnp
from jax import lax
from jax.experimental import pallas as pl
from jax.experimental.pallas import tpu as pltpu
from jax.sharding import PartitionSpec as P

sparsity_weight = 0.4
MESH = pl.DeviceIdType.MESH
F32 = jnp.float32
BF16 = jnp.bfloat16


PLAN_END = (
    "c10", "r00", "r01", "c11", "d00", "c20", "c21", "E00", "E01", "c31", "d01", "C00",
    "C01", "E20", "E11", "E10", "c30", "C20", "r31", "C11", "E21", "r30", "C10", "C21",
    "E31", "C31", "F20", "F21", "E30", "F10", "F11", "F31", "U21", "C30", "F00", "U11",
    "U20", "U31", "F01", "F30", "U10", "U30", "X1", "X0", "R01", "K11", "R00", "K10",
    "D01", "K21", "D00", "K31", "V0", "G0", "K30", "K20", "G1", "R30", "R31", "V1",
    "H0", "G2", "H1", "G3", "V2", "V3", "H2", "H3",
)
PLAN_MID = (
    "r10", "c20", "r11", "c21", "c01", "d10", "c00", "E00", "c31", "d20", "E01", "d11",
    "C00", "c30", "C01", "E20", "d21", "E11", "r31", "E10", "C20", "r30", "C11", "E21",
    "C10", "F20", "C21", "E31", "F01", "C31", "U20", "F21", "E30", "F00", "U01", "F10",
    "F31", "U21", "C30", "U00", "F11", "U31", "F30", "U30", "X1", "X0", "R11", "R10",
    "K01", "K21", "D11", "K00", "K31", "V0", "K20", "K30", "D10", "D21", "G0", "R31",
    "D20", "G1", "R30", "V1", "H0", "G2", "H1", "G3", "V2", "V3", "H2", "H3",
)
ORDERS = ((0, 1, 2, 3), (1, 0, 2, 3))
CORNER_UP = ({0: (1,)}, {1: (1, -1), 2: (-1,)})


def plain_step(activations, enc_weight, enc_bias, dec_weight, dec_bias, active_mask):
    local_rows = activations[0]
    encoder = enc_weight[0]
    decoder = dec_weight[0]
    token_all = lax.all_gather(local_rows, "latent", axis=0, tiled=True)
    layer_pre = jnp.dot(token_all, encoder, preferred_element_type=jnp.float32)
    dec_float = decoder.astype(jnp.float32)
    row_norm = jnp.sqrt(jnp.sum(dec_float * dec_float, axis=1) + 1e-06)
    preact, norm_sum = lax.psum((layer_pre, row_norm), "layer")
    preact = preact + enc_bias
    gating = active_mask.astype(jnp.float32)
    latent_code = preact * gating
    code_b = latent_code.astype(jnp.bfloat16)
    layer_index = lax.axis_index("layer")
    recon_share = (
        lax.psum_scatter(
            jnp.dot(code_b, decoder, preferred_element_type=jnp.float32),
            "latent",
            scatter_dimension=0,
            tiled=True,
        )
        + dec_bias[0]
    )
    error_share = recon_share - local_rows.astype(jnp.float32)
    square_part = 0.5 * jnp.sum(error_share * error_share)
    error_b = lax.all_gather(error_share.astype(jnp.bfloat16), "latent", axis=0, tiled=True)
    layer_grad = jnp.einsum("td,fd->tf", error_b, decoder, preferred_element_type=jnp.float32)
    code_grad = lax.psum(layer_grad, "layer") + sparsity_weight * norm_sum
    preact_grad = (code_grad * gating).astype(jnp.bfloat16)
    grad_enc = jnp.einsum(
        "td,tf->df", token_all, preact_grad, preferred_element_type=jnp.float32
    ).astype(jnp.bfloat16)
    code_total = jnp.sum(latent_code, axis=0)
    shrink = sparsity_weight * code_total[:, None] * dec_float / row_norm[:, None]
    grad_dec = (
        jnp.einsum("tf,td->fd", code_b, error_b, preferred_element_type=jnp.float32) + shrink
    ).astype(jnp.bfloat16)
    sparse_part = jnp.where(
        layer_index == 0, sparsity_weight * jnp.sum(latent_code * norm_sum), 0.0
    )
    loss_total = lax.psum(square_part + sparse_part, ("layer", "latent"))
    loss_value = loss_total / (active_mask.shape[0] * token_all.shape[1])
    return (grad_enc[None], grad_dec[None], loss_value)


def exchange_kernel(n, group, plans, act, enc_hbm, bias, dec_hbm, dbias, mask_hbm,
                    tok_out, pg_out, dec_low, dec_high, loss_out,
                    enc, dec, mask, tok, pre_own, pre_recv, code,
                    rs_send, rs_recv, rs_half, up_send, up_recv, err, lg_own, lg_recv, pg,
                    norm_own, norm_recv, total, coef, acc, gdec, loss_all, load_sem, out_sem,
                    send_sem, ag_r, er_r, rs_s, rs_r, rs_hr, up_s, up_r,
                    pre_s, pre_r, lg_s, lg_r, nm_s, nm_r, ls_s, ls_r):
    me = lax.axis_index("latent")
    layer = lax.axis_index("layer")
    other = 1 - layer
    rows, width = act.shape
    latents = mask.shape[2]
    tokens = n * rows
    span = group * rows
    groups = n // group
    mine = me // group
    spot = lax.rem(me, group)
    low = mine < groups // 2
    at_end = (mine == 0) | (mine == groups - 1)
    toward = jnp.where(low, 1, -1)

    def plane(q):
        return jnp.where(low, q, groups - 1 - q)

    def place(step):
        return plane(jnp.where(at_end, ORDERS[0][step], ORDERS[1][step]))

    side_x = spot ^ 1
    side_y = spot ^ 2
    corner = spot ^ 3
    sides = (side_x, side_y)
    half_rows = rows // 2
    half_span = span // 2

    def half(k):
        return pl.ds(k * half_rows, half_rows)

    def block_of(g):
        return pl.ds(g * group, group)

    loads = [
        pltpu.make_async_copy(hbm, vmem, load_sem.at[i])
        for i, (hbm, vmem) in enumerate(((dec_hbm, dec), (enc_hbm, enc), (mask_hbm, mask)))
    ]
    for load in loads:
        load.start()

    barrier = pltpu.get_barrier_semaphore()
    others = [lax.rem(mine + k, groups) * group + spot for k in range(1, groups)]
    partners = [mine * group + side_x, mine * group + side_y] + others
    for partner in partners:
        pl.semaphore_signal(barrier, inc=1, device_id={"latent": partner}, device_id_type=MESH)
    pl.semaphore_signal(barrier, inc=1, device_id={"layer": other}, device_id_type=MESH)
    pl.semaphore_wait(barrier, len(partners) + 1)

    def latent_copy(src, dst, send, recv, target):
        return pltpu.make_async_remote_copy(
            src_ref=src, dst_ref=dst, send_sem=send, recv_sem=recv,
            device_id={"latent": target}, device_id_type=MESH)

    def layer_copy(src, dst, send, recv):
        return pltpu.make_async_remote_copy(
            src_ref=src, dst_ref=dst, send_sem=send, recv_sem=recv,
            device_id={"layer": other}, device_id_type=MESH)

    class Gather:
        def __init__(self, buf, first, recv_sem):
            self.buf, self.first, self.recv_sem = buf, first, recv_sem
            self.started = ([], [])
            self.seen = (set(), set())

        def piece(self, q, where, k):
            return self.buf.at[plane(q) * group + where, half(k)]

        def wait(self, role, q, where, k, key):
            if (key, q, k) in self.seen[role]:
                return
            self.seen[role].add((key, q, k))
            part = self.piece(q, where, k)
            latent_copy(
                part, part, send_sem.at[0],
                self.recv_sem.at[plane(q) * group + where, k], me).wait_recv()

        def send(self, role, q, where, k, target, own=False):
            index = len(self.started[role])

            def make():
                part = self.piece(q, where, k)
                return latent_copy(
                    self.first.at[half(k)] if own else part, part, send_sem.at[index],
                    self.recv_sem.at[plane(q) * group + where, k], target())

            make().start()
            self.started[role].append(make)

        def along(self, role, q, where, k, shift, own=False):
            self.send(role, q, where, k, lambda: me + shift * toward * group, own)

        def across(self, role, q, k, own=False):
            for to in sides:
                self.send(role, q, spot, k, lambda to=to: mine * group + to, own)

        def run(self, role, event, q, k):
            if event == "o":
                self.across(role, q, k, own=True)
                for shift in ((1,), (1, -1))[role]:
                    self.along(role, q, spot, k, shift, own=True)
            elif event == "c":
                self.wait(role, q, spot, k, "s")
                if role == 1:
                    self.along(role, q, spot, k, 1 if q == 0 else -1)
                self.across(role, q, k)
            elif event == "r":
                self.wait(role, q, sides[k], k, "xy"[k])
                self.send(role, q, sides[k], k, lambda: mine * group + sides[1 - k])
            else:
                self.wait(role, q, corner, k, "d")
                for shift in CORNER_UP[role].get(q, ()):
                    self.along(role, q, corner, k, shift)

        def settle(self, role, q, k):
            if q != role:
                self.wait(role, q, spot, k, "s")
            self.wait(role, q, side_x, k, "x")
            self.wait(role, q, side_y, k, "y")
            self.wait(role, q, corner, k, "d")

        def finish(self, role):
            for make in self.started[role]:
                make().wait_send()

    tokens_in = Gather(tok, act, ag_r)
    errors_in = Gather(err, err.at[me], er_r)

    def by_role(do):
        @pl.when(at_end)
        def _():
            do(0)

        @pl.when(jnp.logical_not(at_end))
        def _():
            do(1)

    def pre_copy(g, k):
        return layer_copy(pre_own.at[g, k], pre_recv.at[g, k], pre_s.at[g, k], pre_r.at[g, k])

    def lg_copy(g):
        return layer_copy(lg_own.at[g], lg_recv.at[g], lg_s.at[g], lg_r.at[g])

    def corner_copy(g, k):
        return latent_copy(
            rs_send.at[g * group + corner, half(k)], rs_half.at[k, g],
            rs_s.at[2, k, g], rs_hr.at[k, g], mine * group + sides[1 - k])

    def side_copy(g, i, k):
        return latent_copy(
            rs_send.at[g * group + sides[i], half(k)], rs_recv.at[g * group + spot, half(k)],
            rs_s.at[i, k, g], rs_r.at[i, k, g], mine * group + sides[i])

    def side_arrived(g, k):
        for i, source in enumerate(sides):
            part = rs_recv.at[g * group + source, half(k)]
            latent_copy(part, part, rs_s.at[i, k, g], rs_r.at[i, k, g], me).wait_recv()

    def up_copy(g, k):
        return latent_copy(
            up_send.at[g, half(k)], up_recv.at[mine, half(k)],
            up_s.at[k, g], up_r.at[k, mine], g * group + spot)

    def up_arrived(g, k):
        part = up_recv.at[g, half(k)]
        latent_copy(part, part, up_s.at[k, g], up_r.at[k, g], me).wait_recv()

    tile = min(512, latents)
    wide = min(512, width)
    lanes = 128

    def norm_block(block, carry):
        at = pl.multiple_of(block * lanes, lanes)
        piece = dec[pl.ds(at, lanes), :].astype(F32)
        sums = jnp.sum(piece * piece, axis=1, keepdims=True)
        norm = jnp.sqrt(sums + 1e-06)
        norm_own[:, pl.ds(at, lanes)] = jnp.broadcast_to(norm, (lanes, lanes)).T[0:8, :]
        return carry

    norm_copy = layer_copy(norm_own, norm_recv, nm_s, nm_r)

    def encode(step, k):
        g = place(step)
        left = tok[block_of(g), half(k)].reshape(half_span, width)
        for c in range(latents // tile):
            cols = pl.ds(c * tile, tile)
            pre_own[g, k, :, cols] = jnp.dot(left, enc[:, cols], preferred_element_type=F32)
        pre_copy(g, k).start()

    def decode(step, k):
        g = place(step)
        pre_copy(g, k).wait_recv()
        for c in range(latents // tile):
            cols = pl.ds(c * tile, tile)
            gating = mask[block_of(g), half(k), cols].reshape(half_span, tile).astype(F32)
            preact = pre_own[g, k, :, cols] + pre_recv[g, k, :, cols] + bias[0:1, cols]
            latent = preact * gating
            total[0:1, cols] += jnp.sum(latent, axis=0, keepdims=True)
            code[block_of(g), half(k), cols] = latent.astype(BF16).reshape(group, half_rows, tile)
        left = code[block_of(g), half(k)].reshape(half_span, latents)
        for c in range(width // wide):
            cols = pl.ds(c * wide, wide)
            part = jnp.dot(left, dec[:, cols], preferred_element_type=F32).astype(BF16)
            rs_send[block_of(g), half(k), cols] = part.reshape(group, half_rows, wide)
        corner_copy(g, k).start()
        side_copy(g, 1 - k, k).start()

    def fold(q, k):
        g = plane(q)
        part = rs_half.at[k, g]
        latent_copy(part, part, rs_s.at[2, k, g], rs_hr.at[k, g], me).wait_recv()
        at = (g * group + sides[k], half(k))
        rs_send[at] = (rs_send[at].astype(F32) + rs_half[k, g].astype(F32)).astype(BF16)
        side_copy(g, k, k).start()

    def plane_sum(g, k, cols):
        part = rs_send[g * group + spot, half(k), cols].astype(F32)
        for source in sides:
            part = part + rs_recv[g * group + source, half(k), cols].astype(F32)
        return part

    def climb(q, k):
        g = plane(q)
        side_arrived(g, k)
        for c in range(width // wide):
            cols = pl.ds(c * wide, wide)
            up_send[g, half(k), cols] = plane_sum(g, k, cols).astype(BF16)
        up_copy(g, k).start()

    squares = []

    def error(k):
        side_arrived(mine, k)
        planes = [lax.rem(mine + j, groups) for j in range(1, groups)]
        for g in planes:
            up_arrived(g, k)
        if not squares:
            by_role(tokens_in.finish)
        for c in range(width // wide):
            cols = pl.ds(c * wide, wide)
            recon = plane_sum(mine, k, cols)
            for g in planes:
                recon = recon + up_recv[g, half(k), cols].astype(F32)
            gap = recon + dbias[0:1, cols] - act[half(k), cols].astype(F32)
            squares.append(jnp.sum(gap * gap))
            err[me, half(k), cols] = gap.astype(BF16)
        by_role(lambda role: errors_in.run(role, "o", role, k))
        if len(squares) == 2 * (width // wide):
            settle_sums()

    def loss_copy(index, source, slot, target):
        return latent_copy(
            loss_all.at[source], loss_all.at[slot], ls_s.at[index], ls_r.at[slot], target)

    def loss_z(j):
        return loss_copy(j + 1, 4, 5 + mine, others[j - 1])

    def loss_pair():
        return layer_copy(loss_all.at[9], loss_all.at[10], ls_s.at[5], ls_r.at[10])

    def settle_sums():
        tok_copy.start()
        norm_copy.wait()
        norm_sum = norm_own[0:1, :] + norm_recv[0:1, :]
        sparse = sparsity_weight * jnp.sum(total[0:1, :] * norm_sum)
        ratio = sparsity_weight * total[0:1, :] / norm_own[0:1, :]
        coef[...] = jnp.broadcast_to(ratio, (lanes, latents)).T
        norm_recv[...] = jnp.broadcast_to(sparsity_weight * norm_sum, norm_recv.shape)
        partial = 0.5 * sum(squares) + jnp.where(layer == 0, sparse, 0.0)
        loss_all[0] = jnp.broadcast_to(partial, loss_all.shape[1:])
        loss_copy(0, 0, 1, partners[0]).start()

    def loss_step(step):
        if step == 0:
            loss_copy(0, 0, 1, partners[0]).wait()
            loss_all[2] = loss_all[0] + loss_all[1]
            loss_copy(1, 2, 3, partners[1]).start()
        elif step == 1:
            loss_copy(1, 2, 3, partners[1]).wait()
            loss_all[4] = loss_all[2] + loss_all[3]
            loss_all[5 + mine] = loss_all[4]
            for j in range(1, groups):
                loss_z(j).start()
        elif step == 2:
            for j in range(1, groups):
                latent_copy(
                    loss_all.at[4], loss_all.at[5 + lax.rem(mine + j, groups)],
                    ls_s.at[j + 1], ls_r.at[5 + lax.rem(mine + j, groups)], me).wait_recv()
                loss_z(j).wait_send()
            loss_all[9] = loss_all[5] + loss_all[6] + loss_all[7] + loss_all[8]
            loss_pair().start()
        else:
            loss_pair().wait()
            loss_out[...] = (loss_all[9] + loss_all[10]) / (tokens * width)

    def grad(step, k):
        g = place(step)
        left = err[block_of(g)].reshape(span, width)
        for c in range(latents // tile):
            cols = pl.ds(c * tile, tile)
            lg_own[g, :, cols] = lax.dot_general(
                left, dec[cols, :], (((1,), (1,)), ((), ())), preferred_element_type=F32)
        lg_copy(g).start()
        loss_step(step)

    def gate(step, k):
        g = place(step)
        lg_copy(g).wait_recv()
        for c in range(latents // tile):
            cols = pl.ds(c * tile, tile)
            gating = mask[block_of(g), :, cols].reshape(span, tile).astype(F32)
            code_grad = lg_own[g, :, cols] + lg_recv[g, :, cols] + norm_recv[0:1, cols]
            pg[block_of(g), :, cols] = (code_grad * gating).astype(BF16).reshape(group, rows, tile)
        pg_copy(g).start()

    def pg_copy(g):
        return pltpu.make_async_copy(pg.at[block_of(g)], pg_out.at[block_of(g)], out_sem.at[1 + g])

    def dec_copy(c):
        cols = pl.ds(c * wide, wide)
        part = width // 2
        out = (dec_low, dec_high)[c * wide // part]
        return pltpu.make_async_copy(
            gdec.at[:, cols], out.at[:, pl.ds(c * wide % part, wide)], out_sem.at[1 + groups + c])

    def outer(step, k):
        g = place(step)
        left = code[block_of(g)].reshape(span, latents)
        right = err[block_of(g)].reshape(span, width)
        for c in range(width // wide):
            cols = pl.ds(c * wide, wide)
            part = lax.dot_general(
                left, right[:, c * wide:(c + 1) * wide], (((0,), (0,)), ((), ())),
                preferred_element_type=F32)
            if step == 0:
                acc[:, cols] = part + coef[:, 0:1] * dec[:, cols].astype(F32)
            elif step < groups - 1:
                acc[:, cols] += part
            else:
                gdec[:, cols] = (acc[:, cols] + part).astype(BF16)
                dec_copy(c).start()

    tok_copy = pltpu.make_async_copy(tok, tok_out, out_sem.at[0])

    def open_tokens(k):
        by_role(lambda role: tokens_in.run(role, "o", role, k))

    for k in range(2):
        open_tokens(k)
    tok[me] = act[...]
    loads[0].wait()
    lax.fori_loop(0, latents // lanes, norm_block, 0)
    norm_copy.start()
    total[...] = jnp.zeros_like(total)
    loads[1].wait()
    loads[2].wait()

    steps = {"E": encode, "C": decode, "X": error, "G": grad, "V": outer, "H": gate}
    taken = [0, 0]

    def between(role, token):
        plan = plans[role]
        while taken[role] < len(plan) and plan[taken[role]][0] not in steps:
            event = plan[taken[role]]
            q, k = int(event[1]), int(event[2])
            if event[0] == "F":
                fold(q, k)
            elif event[0] == "U":
                climb(q, k)
            elif event[0] in "crd":
                tokens_in.run(role, event[0], q, k)
            else:
                errors_in.run(role, event[0].lower().replace("k", "c"), q, k)
            taken[role] += 1
        taken[role] += 1
        if token and token[0] == "E":
            tokens_in.settle(role, ORDERS[role][int(token[1])], int(token[2]))
        elif token and token[0] in "GV":
            for k in range(2):
                errors_in.settle(role, ORDERS[role][int(token[1])], k)

    for token in [token for token in plans[0] if token[0] in steps] + [""]:
        by_role(lambda role: between(role, token))
        if token and token[0] == "X":
            error(int(token[1]))
        elif token:
            steps[token[0]](int(token[1]), int(token[2]) if len(token) > 2 else 0)

    by_role(errors_in.finish)

    def finish_group(g, carry):
        lg_copy(g).wait_send()
        pg_copy(g).wait()
        for k in range(2):
            pre_copy(g, k).wait_send()
            corner_copy(g, k).wait_send()
            for i in range(2):
                side_copy(g, i, k).wait_send()
        return carry

    lax.fori_loop(0, groups, finish_group, 0)
    for j in range(1, groups):
        for k in range(2):
            up_copy(lax.rem(mine + j, groups), k).wait_send()
    for c in range(width // wide):
        dec_copy(c).wait()
    tok_copy.wait()


def grads_kernel(tok, pg, dec_low, dec_high, loss, enc_out, dec_out, loss_out, sem):
    step = pl.program_id(0)
    part = dec_low.shape[1]
    copies = [
        pltpu.make_async_copy(half, dec_out.at[:, pl.ds(i * part, part)], sem.at[i])
        for i, half in enumerate((dec_low, dec_high))
    ]

    @pl.when(step == 0)
    def _():
        for copy in copies:
            copy.start()
        loss_out[...] = loss[0:1, 0:1]

    enc_out[...] = lax.dot_general(
        tok[...], pg[...], (((0,), (0,)), ((), ())), preferred_element_type=F32).astype(BF16)

    @pl.when(step == pl.num_programs(0) - 1)
    def _():
        for copy in copies:
            copy.wait()


def fast_step(n, activations, enc_weight, enc_bias, dec_weight, dec_bias, active_mask):
    rows, width = activations.shape[1:]
    tokens, latents = active_mask.shape
    group = 4
    groups = n // group
    span = group * rows
    decoder = dec_weight[0]
    vmem = pl.BlockSpec(memory_space=pltpu.VMEM)
    anyw = pl.BlockSpec(memory_space=pl.ANY)
    shape = jax.ShapeDtypeStruct
    dma = pltpu.SemaphoreType.DMA
    tok, pg, dec_low, dec_high, loss = pl.pallas_call(
        functools.partial(exchange_kernel, n, group, (PLAN_END, PLAN_MID)),
        out_shape=(
            shape((n, rows, width), BF16),
            shape((n, rows, latents), BF16),
            shape((latents, width // 2), BF16),
            shape((latents, width // 2), BF16),
            shape((8, 128), F32),
        ),
        in_specs=[vmem, anyw, vmem, anyw, vmem, anyw],
        out_specs=(anyw, anyw, anyw, anyw, vmem),
        scratch_shapes=[
            pltpu.VMEM((width, latents), BF16),
            pltpu.VMEM((latents, width), BF16),
            pltpu.VMEM((n, rows, latents), jnp.int32),
            pltpu.VMEM((n, rows, width), BF16),
            pltpu.VMEM((groups, 2, span // 2, latents), F32),
            pltpu.VMEM((groups, 2, span // 2, latents), F32),
            pltpu.VMEM((n, rows, latents), BF16),
            pltpu.VMEM((n, rows, width), BF16),
            pltpu.VMEM((n, rows, width), BF16),
            pltpu.VMEM((2, groups, rows // 2, width), BF16),
            pltpu.VMEM((groups, rows, width), BF16),
            pltpu.VMEM((groups, rows, width), BF16),
            pltpu.VMEM((n, rows, width), BF16),
            pltpu.VMEM((groups, span, latents), F32),
            pltpu.VMEM((groups, span, latents), F32),
            pltpu.VMEM((n, rows, latents), BF16),
            pltpu.VMEM((8, latents), F32),
            pltpu.VMEM((8, latents), F32),
            pltpu.VMEM((8, latents), F32),
            pltpu.VMEM((latents, 128), F32),
            pltpu.VMEM((latents, width), F32),
            pltpu.VMEM((latents, width), BF16),
            pltpu.VMEM((11, 8, 128), F32),
            dma((3,)), dma((1 + groups + width // min(512, width),)),
            dma((36,)), dma((n, 2)), dma((n, 2)),
            dma((3, 2, groups)), dma((2, 2, groups)), dma((2, groups)),
            dma((2, groups)), dma((2, groups)),
            dma((groups, 2)), dma((groups, 2)), dma((groups,)), dma((groups,)),
            dma, dma, dma((6,)), dma((11,)),
        ],
        compiler_params=pltpu.CompilerParams(
            collective_id=0, has_side_effects=True, vmem_limit_bytes=45 << 20),
    )(activations[0], enc_weight[0], enc_bias[None], decoder, dec_bias,
      active_mask.reshape(n, rows, latents))
    tile = min(256, latents)
    grad_enc, grad_dec, loss = pl.pallas_call(
        grads_kernel,
        grid=(latents // tile,),
        out_shape=(
            shape((width, latents), BF16),
            shape((latents, width), BF16),
            shape((1, 1), F32),
        ),
        in_specs=[
            vmem,
            pl.BlockSpec((tokens, tile), lambda i: (0, i)),
            anyw,
            anyw,
            vmem,
        ],
        out_specs=(
            pl.BlockSpec((width, tile), lambda i: (0, i)),
            anyw,
            pl.BlockSpec((1, 1), lambda i: (0, 0)),
        ),
        scratch_shapes=[dma((2,))],
        compiler_params=pltpu.CompilerParams(vmem_limit_bytes=12 << 20),
    )(tok.reshape(tokens, width), pg.reshape(tokens, latents), dec_low, dec_high, loss)
    return (grad_enc[None], grad_dec[None], loss.reshape(()))


def solution(mesh):
    placed = (
        P("layer", "latent", None),
        P("layer", None, "latent"),
        P("latent"),
        P("layer", "latent", None),
        P("layer", None),
        P(None, "latent"),
    )
    n = mesh.shape["latent"]

    def per_device(activations, *others):
        rows = activations.shape[1]
        if rows == 32 and n == 16:
            return fast_step(n, activations, *others)
        return plain_step(activations, *others)

    return jax.shard_map(
        per_device,
        mesh=mesh,
        in_specs=placed,
        out_specs=(P("layer", None, "latent"), P("layer", "latent", None), P()),
        check_vma=False,
    )
```

```python
import functools

import jax
import jax.numpy as jnp
from jax import lax
from jax.experimental import pallas as pl
from jax.experimental.pallas import tpu as pltpu
from jax.sharding import PartitionSpec as P

sparsity_weight = 0.4
MESH = pl.DeviceIdType.MESH
F32 = jnp.float32
BF16 = jnp.bfloat16


PLAN_END = (
    "r00", "c10", "r01", "d00", "c11", "c20", "E01", "d01", "c30", "E00", "C01", "E10",
    "c31", "r30", "E11", "c21", "r31", "C10", "E20", "C11", "C20", "E30", "E21", "F10",
    "C30", "F20", "C21", "F11", "C00", "E31", "U20", "F30", "C31", "U10", "U11", "F21",
    "U30", "F31", "F00", "U21", "U31", "F01", "X0", "R00", "X1", "K10", "R01", "K11",
    "D00", "K20", "D01", "K21", "G0", "K30", "V0", "H0", "K31", "G1", "R30", "V1",
    "R31", "G2", "V2", "H1", "H2", "G3", "V3", "H3",
)
PLAN_MID = (
    "c00", "r10", "r11", "c20", "c01", "c30", "d10", "c31", "d11", "E01", "E00", "C01",
    "E10", "c21", "E11", "r30", "d20", "r31", "C10", "E20", "C11", "d21", "C20", "E30",
    "E21", "C30", "F00", "F20", "C21", "C00", "F30", "E31", "F21", "C31", "U20", "U30",
    "F01", "U21", "F31", "F11", "F10", "U00", "U01", "U31", "X0", "R10", "X1", "K00",
    "D10", "K20", "R11", "K21", "K01", "K30", "D11", "G0", "K31", "V0", "D21", "R30",
    "H0", "D20", "G1", "R31", "V1", "G2", "V2", "H1", "H2", "G3", "V3", "H3",
)
ORDERS = ((0, 1, 2, 3), (1, 0, 2, 3))
CORNER_UP = ({0: (1,)}, {1: (1, -1), 2: (-1,)})


def plain_step(activations, enc_weight, enc_bias, dec_weight, dec_bias, active_mask):
    local_rows = activations[0]
    encoder = enc_weight[0]
    decoder = dec_weight[0]
    token_all = lax.all_gather(local_rows, "latent", axis=0, tiled=True)
    layer_pre = jnp.dot(token_all, encoder, preferred_element_type=jnp.float32)
    dec_float = decoder.astype(jnp.float32)
    row_norm = jnp.sqrt(jnp.sum(dec_float * dec_float, axis=1) + 1e-06)
    preact, norm_sum = lax.psum((layer_pre, row_norm), "layer")
    preact = preact + enc_bias
    gating = active_mask.astype(jnp.float32)
    latent_code = preact * gating
    code_b = latent_code.astype(jnp.bfloat16)
    layer_index = lax.axis_index("layer")
    recon_share = (
        lax.psum_scatter(
            jnp.dot(code_b, decoder, preferred_element_type=jnp.float32),
            "latent",
            scatter_dimension=0,
            tiled=True,
        )
        + dec_bias[0]
    )
    error_share = recon_share - local_rows.astype(jnp.float32)
    square_part = 0.5 * jnp.sum(error_share * error_share)
    error_b = lax.all_gather(error_share.astype(jnp.bfloat16), "latent", axis=0, tiled=True)
    layer_grad = jnp.einsum("td,fd->tf", error_b, decoder, preferred_element_type=jnp.float32)
    code_grad = lax.psum(layer_grad, "layer") + sparsity_weight * norm_sum
    preact_grad = (code_grad * gating).astype(jnp.bfloat16)
    grad_enc = jnp.einsum(
        "td,tf->df", token_all, preact_grad, preferred_element_type=jnp.float32
    ).astype(jnp.bfloat16)
    code_total = jnp.sum(latent_code, axis=0)
    shrink = sparsity_weight * code_total[:, None] * dec_float / row_norm[:, None]
    grad_dec = (
        jnp.einsum("tf,td->fd", code_b, error_b, preferred_element_type=jnp.float32) + shrink
    ).astype(jnp.bfloat16)
    sparse_part = jnp.where(
        layer_index == 0, sparsity_weight * jnp.sum(latent_code * norm_sum), 0.0
    )
    loss_total = lax.psum(square_part + sparse_part, ("layer", "latent"))
    loss_value = loss_total / (active_mask.shape[0] * token_all.shape[1])
    return (grad_enc[None], grad_dec[None], loss_value)


def exchange_kernel(n, group, plans, act, enc_hbm, bias, dec_hbm, dbias, mask_hbm,
                    tok_out, pg_out, dec_low, dec_high, loss_out,
                    enc, dec, mask, tok, pre_own, pre_recv, code,
                    rs_send, rs_recv, rs_half, up_send, up_recv, err, lg_own, lg_recv, pg,
                    norm_own, norm_recv, total, coef, acc, gdec, loss_all, load_sem, out_sem,
                    gather_sem, sum_sem, ag_r, er_r, rs_r, rs_hr, up_r,
                    pair_r, nm_s, nm_r, ls_s, ls_r):
    me = lax.axis_index("latent")
    layer = lax.axis_index("layer")
    other = 1 - layer
    rows, width = act.shape
    latents = mask.shape[2]
    tokens = n * rows
    span = group * rows
    groups = n // group
    mine = me // group
    spot = lax.rem(me, group)
    low = mine < groups // 2
    at_end = (mine == 0) | (mine == groups - 1)
    toward = jnp.where(low, 1, -1)

    def plane(q):
        return jnp.where(low, q, groups - 1 - q)

    def place(step):
        return plane(jnp.where(at_end, ORDERS[0][step], ORDERS[1][step]))

    side_x = spot ^ 1
    side_y = spot ^ 2
    corner = spot ^ 3
    sides = (side_x, side_y)
    half_rows = rows // 2
    half_span = span // 2

    def half(k):
        return pl.ds(k * half_rows, half_rows)

    def block_of(g):
        return pl.ds(g * group, group)

    loads = [
        pltpu.make_async_copy(hbm, vmem, load_sem.at[i])
        for i, (hbm, vmem) in enumerate(((dec_hbm, dec), (enc_hbm, enc), (mask_hbm, mask)))
    ]
    for load in loads:
        load.start()

    barrier = pltpu.get_barrier_semaphore()
    others = [lax.rem(mine + k, groups) * group + spot for k in range(1, groups)]
    partners = [mine * group + side_x, mine * group + side_y] + others
    for partner in partners:
        pl.semaphore_signal(barrier, inc=1, device_id={"latent": partner}, device_id_type=MESH)
    pl.semaphore_signal(barrier, inc=1, device_id={"layer": other}, device_id_type=MESH)
    pl.semaphore_wait(barrier, len(partners) + 1)

    def latent_copy(src, dst, send, recv, target):
        return pltpu.make_async_remote_copy(
            src_ref=src, dst_ref=dst, send_sem=send, recv_sem=recv,
            device_id={"latent": target}, device_id_type=MESH)

    def layer_copy(src, dst, send, recv):
        return pltpu.make_async_remote_copy(
            src_ref=src, dst_ref=dst, send_sem=send, recv_sem=recv,
            device_id={"layer": other}, device_id_type=MESH)

    class Gather:
        def __init__(self, buf, first, recv_sem):
            self.buf, self.first, self.recv_sem = buf, first, recv_sem
            self.started = [0, 0]
            self.seen = (set(), set())

        def piece(self, q, where, k):
            return self.buf.at[plane(q) * group + where, half(k)]

        def wait(self, role, q, where, k, key):
            if (key, q, k) in self.seen[role]:
                return
            self.seen[role].add((key, q, k))
            part = self.piece(q, where, k)
            latent_copy(
                part, part, gather_sem,
                self.recv_sem.at[plane(q) * group + where, k], me).wait_recv()

        def send(self, role, q, where, k, target, own=False):
            part = self.piece(q, where, k)
            latent_copy(
                self.first.at[half(k)] if own else part, part, gather_sem,
                self.recv_sem.at[plane(q) * group + where, k], target()).start()
            self.started[role] += 1

        def along(self, role, q, where, k, shift, own=False):
            self.send(role, q, where, k, lambda: me + shift * toward * group, own)

        def across(self, role, q, k, own=False):
            for to in sides:
                self.send(role, q, spot, k, lambda to=to: mine * group + to, own)

        def run(self, role, event, q, k):
            if event == "o":
                self.across(role, q, k, own=True)
                for shift in ((1,), (1, -1))[role]:
                    self.along(role, q, spot, k, shift, own=True)
            elif event == "c":
                self.wait(role, q, spot, k, "s")
                if role == 1:
                    self.along(role, q, spot, k, 1 if q == 0 else -1)
                self.across(role, q, k)
            elif event == "r":
                self.wait(role, q, sides[k], k, "xy"[k])
                self.send(role, q, sides[k], k, lambda: mine * group + sides[1 - k])
            else:
                self.wait(role, q, corner, k, "d")
                for shift in CORNER_UP[role].get(q, ()):
                    self.along(role, q, corner, k, shift)

        def settle(self, role, q, k):
            if q != role:
                self.wait(role, q, spot, k, "s")
            self.wait(role, q, side_x, k, "x")
            self.wait(role, q, side_y, k, "y")
            self.wait(role, q, corner, k, "d")

    tokens_in = Gather(tok, act, ag_r)
    errors_in = Gather(err, err.at[me], er_r)

    def by_role(do):
        @pl.when(at_end)
        def _():
            do(0)

        @pl.when(jnp.logical_not(at_end))
        def _():
            do(1)

    def pre_copy(g, k):
        return layer_copy(pre_own.at[g, k], pre_recv.at[g, k], sum_sem, pair_r.at[g, k])

    def lg_copy(g):
        return layer_copy(lg_own.at[g], lg_recv.at[g], sum_sem, pair_r.at[g, 0])

    def corner_copy(g, k):
        return latent_copy(
            rs_send.at[g * group + corner, half(k)], rs_half.at[k, g],
            sum_sem, rs_hr.at[k, g], mine * group + sides[1 - k])

    def side_copy(g, i, k):
        return latent_copy(
            rs_send.at[g * group + sides[i], half(k)], rs_recv.at[g * group + spot, half(k)],
            sum_sem, rs_r.at[k, g], mine * group + sides[i])

    def pieces(count):
        return acc.at[pl.ds(0, count * half_rows // 2)]

    def side_arrived(g, k):
        part = pieces(2)
        latent_copy(part, part, sum_sem, rs_r.at[k, g], me).wait_recv()

    def up_copy(g, k):
        return latent_copy(
            up_send.at[g, half(k)], up_recv.at[mine, half(k)],
            sum_sem, up_r.at[k], g * group + spot)

    def up_arrived(k):
        part = pieces(groups - 1)
        latent_copy(part, part, sum_sem, up_r.at[k], me).wait_recv()

    tile = min(512, latents)
    wide = min(512, width)
    lanes = 128

    def norm_block(block, carry):
        at = pl.multiple_of(block * lanes, lanes)
        piece = dec[pl.ds(at, lanes), :].astype(F32)
        sums = jnp.sum(piece * piece, axis=1, keepdims=True)
        norm = jnp.sqrt(sums + 1e-06)
        norm_own[:, pl.ds(at, lanes)] = jnp.broadcast_to(norm, (lanes, lanes)).T[0:8, :]
        return carry

    norm_copy = layer_copy(norm_own, norm_recv, nm_s, nm_r)

    def encode(step, k):
        g = place(step)
        left = tok[block_of(g), half(k)].reshape(half_span, width)
        for c in range(latents // tile):
            cols = pl.ds(c * tile, tile)
            pre_own[g, k, :, cols] = jnp.dot(left, enc[:, cols], preferred_element_type=F32)
        pre_copy(g, k).start()

    def decode(step, k):
        g = place(step)
        pre_copy(g, k).wait_recv()
        for c in range(latents // tile):
            cols = pl.ds(c * tile, tile)
            gating = mask[block_of(g), half(k), cols].reshape(half_span, tile).astype(F32)
            preact = pre_own[g, k, :, cols] + pre_recv[g, k, :, cols] + bias[0:1, cols]
            latent = preact * gating
            total[0:1, cols] += jnp.sum(latent, axis=0, keepdims=True)
            code[block_of(g), half(k), cols] = latent.astype(BF16).reshape(group, half_rows, tile)
        left = code[block_of(g), half(k)].reshape(half_span, latents)
        for c in range(width // wide):
            cols = pl.ds(c * wide, wide)
            part = jnp.dot(left, dec[:, cols], preferred_element_type=F32).astype(BF16)
            rs_send[block_of(g), half(k), cols] = part.reshape(group, half_rows, wide)
        corner_copy(g, k).start()
        side_copy(g, 1 - k, k).start()

    def fold(q, k):
        g = plane(q)
        part = rs_half.at[k, g]
        latent_copy(part, part, sum_sem, rs_hr.at[k, g], me).wait_recv()
        at = (g * group + sides[k], half(k))
        rs_send[at] = (rs_send[at].astype(F32) + rs_half[k, g].astype(F32)).astype(BF16)
        side_copy(g, k, k).start()

    def plane_sum(g, k, cols):
        part = rs_send[g * group + spot, half(k), cols].astype(F32)
        for source in sides:
            part = part + rs_recv[g * group + source, half(k), cols].astype(F32)
        return part

    def climb(q, k):
        g = plane(q)
        side_arrived(g, k)
        for c in range(width // wide):
            cols = pl.ds(c * wide, wide)
            up_send[g, half(k), cols] = plane_sum(g, k, cols).astype(BF16)
        up_copy(g, k).start()

    squares = []

    def error(k):
        side_arrived(mine, k)
        planes = [lax.rem(mine + j, groups) for j in range(1, groups)]
        up_arrived(k)
        for c in range(width // wide):
            cols = pl.ds(c * wide, wide)
            recon = plane_sum(mine, k, cols)
            for g in planes:
                recon = recon + up_recv[g, half(k), cols].astype(F32)
            gap = recon + dbias[0:1, cols] - act[half(k), cols].astype(F32)
            squares.append(jnp.sum(gap * gap))
            err[me, half(k), cols] = gap.astype(BF16)
        by_role(lambda role: errors_in.run(role, "o", role, k))
        if len(squares) == 2 * (width // wide):
            settle_sums()

    def loss_copy(index, source, slot, target):
        return latent_copy(
            loss_all.at[source], loss_all.at[slot], ls_s.at[index], ls_r.at[slot], target)

    def loss_z(j):
        return loss_copy(j + 1, 4, 5 + mine, others[j - 1])

    def loss_pair():
        return layer_copy(loss_all.at[9], loss_all.at[10], ls_s.at[5], ls_r.at[10])

    def settle_sums():
        tok_copy.start()
        norm_copy.wait()
        norm_sum = norm_own[0:1, :] + norm_recv[0:1, :]
        sparse = sparsity_weight * jnp.sum(total[0:1, :] * norm_sum)
        ratio = sparsity_weight * total[0:1, :] / norm_own[0:1, :]
        coef[...] = jnp.broadcast_to(ratio, (lanes, latents)).T
        norm_recv[...] = jnp.broadcast_to(sparsity_weight * norm_sum, norm_recv.shape)
        partial = 0.5 * sum(squares) + jnp.where(layer == 0, sparse, 0.0)
        loss_all[0] = jnp.broadcast_to(partial, loss_all.shape[1:])
        loss_copy(0, 0, 1, partners[0]).start()

    def loss_step(step):
        if step == 0:
            loss_copy(0, 0, 1, partners[0]).wait()
            loss_all[2] = loss_all[0] + loss_all[1]
            loss_copy(1, 2, 3, partners[1]).start()
        elif step == 1:
            loss_copy(1, 2, 3, partners[1]).wait()
            loss_all[4] = loss_all[2] + loss_all[3]
            loss_all[5 + mine] = loss_all[4]
            for j in range(1, groups):
                loss_z(j).start()
        elif step == 2:
            for j in range(1, groups):
                latent_copy(
                    loss_all.at[4], loss_all.at[5 + lax.rem(mine + j, groups)],
                    ls_s.at[j + 1], ls_r.at[5 + lax.rem(mine + j, groups)], me).wait_recv()
                loss_z(j).wait_send()
            loss_all[9] = loss_all[5] + loss_all[6] + loss_all[7] + loss_all[8]
            loss_pair().start()
        else:
            loss_pair().wait()
            loss_out[...] = (loss_all[9] + loss_all[10]) / (tokens * width)

    def grad(step, k):
        g = place(step)
        left = err[block_of(g)].reshape(span, width)
        for c in range(latents // tile):
            cols = pl.ds(c * tile, tile)
            lg_own[g, :, cols] = lax.dot_general(
                left, dec[cols, :], (((1,), (1,)), ((), ())), preferred_element_type=F32)
        lg_copy(g).start()
        loss_step(step)

    def gate(step, k):
        g = place(step)
        lg_copy(g).wait_recv()
        for c in range(latents // tile):
            cols = pl.ds(c * tile, tile)
            gating = mask[block_of(g), :, cols].reshape(span, tile).astype(F32)
            code_grad = lg_own[g, :, cols] + lg_recv[g, :, cols] + norm_recv[0:1, cols]
            pg[block_of(g), :, cols] = (code_grad * gating).astype(BF16).reshape(group, rows, tile)
        pg_copy(g).start()

    def pg_copy(g):
        return pltpu.make_async_copy(pg.at[block_of(g)], pg_out.at[block_of(g)], out_sem.at[1 + g])

    def dec_copy(c):
        cols = pl.ds(c * wide, wide)
        part = width // 2
        out = (dec_low, dec_high)[c * wide // part]
        return pltpu.make_async_copy(
            gdec.at[:, cols], out.at[:, pl.ds(c * wide % part, wide)], out_sem.at[1 + groups + c])

    def outer(step, k):
        g = place(step)
        left = code[block_of(g)].reshape(span, latents)
        right = err[block_of(g)].reshape(span, width)
        for c in range(width // wide):
            cols = pl.ds(c * wide, wide)
            part = lax.dot_general(
                left, right[:, c * wide:(c + 1) * wide], (((0,), (0,)), ((), ())),
                preferred_element_type=F32)
            if step == 0:
                acc[:, cols] = part + coef[:, 0:1] * dec[:, cols].astype(F32)
            elif step < groups - 1:
                acc[:, cols] += part
            else:
                gdec[:, cols] = (acc[:, cols] + part).astype(BF16)
                dec_copy(c).start()

    tok_copy = pltpu.make_async_copy(tok, tok_out, out_sem.at[0])

    def open_tokens(k):
        by_role(lambda role: tokens_in.run(role, "o", role, k))

    for k in range(2):
        open_tokens(k)
    tok[me] = act[...]
    loads[0].wait()
    lax.fori_loop(0, latents // lanes, norm_block, 0)
    norm_copy.start()
    total[...] = jnp.zeros_like(total)
    loads[1].wait()
    loads[2].wait()

    steps = {"E": encode, "C": decode, "X": error, "G": grad, "V": outer, "H": gate}
    taken = [0, 0]

    def between(role, token):
        plan = plans[role]
        while taken[role] < len(plan) and plan[taken[role]][0] not in steps:
            event = plan[taken[role]]
            q, k = int(event[1]), int(event[2])
            if event[0] == "F":
                fold(q, k)
            elif event[0] == "U":
                climb(q, k)
            elif event[0] in "crd":
                tokens_in.run(role, event[0], q, k)
            else:
                errors_in.run(role, event[0].lower().replace("k", "c"), q, k)
            taken[role] += 1
        taken[role] += 1
        if token and token[0] == "E":
            tokens_in.settle(role, ORDERS[role][int(token[1])], int(token[2]))
        elif token and token[0] in "GV":
            for k in range(2):
                errors_in.settle(role, ORDERS[role][int(token[1])], k)

    for token in [token for token in plans[0] if token[0] in steps] + [""]:
        by_role(lambda role: between(role, token))
        if token and token[0] == "X":
            error(int(token[1]))
        elif token:
            steps[token[0]](int(token[1]), int(token[2]) if len(token) > 2 else 0)

    def sent(sem, count):
        part = pieces(count)
        latent_copy(part, part, sem, sem, me).wait_send()

    by_role(lambda role: sent(gather_sem, tokens_in.started[role] + errors_in.started[role]))
    pairs = 2 * groups * span * latents * 4 // (half_rows * width * 2)
    sent(sum_sem, 6 * groups + 2 * (groups - 1) + pairs)

    def finish_group(g, carry):
        pg_copy(g).wait()
        return carry

    lax.fori_loop(0, groups, finish_group, 0)
    for c in range(width // wide):
        dec_copy(c).wait()
    tok_copy.wait()


def grads_kernel(tok, pg, dec_low, dec_high, loss, enc_out, dec_out, loss_out, buf, sem):
    part = dec_low.shape[1]
    copies = [
        pltpu.make_async_copy(half, dec_out.at[:, pl.ds(i * part, part)], sem.at[i])
        for i, half in enumerate((dec_low, dec_high))
    ]
    for copy in copies:
        copy.start()
    loss_out[...] = loss[0:1, 0:1]
    width = tok.shape[1]
    tile = min(512, width)
    for i in range(width // tile):
        here = pl.ds(i * tile, tile)
        buf[here, :] = lax.dot_general(
            tok[:, here], pg[...], (((0,), (0,)), ((), ())), preferred_element_type=F32).astype(BF16)
        copies.append(pltpu.make_async_copy(buf.at[here], enc_out.at[here], sem.at[2 + i]))
        copies[-1].start()
    for copy in copies:
        copy.wait()


def fast_step(n, activations, enc_weight, enc_bias, dec_weight, dec_bias, active_mask):
    rows, width = activations.shape[1:]
    tokens, latents = active_mask.shape
    group = 4
    groups = n // group
    span = group * rows
    decoder = dec_weight[0]
    vmem = pl.BlockSpec(memory_space=pltpu.VMEM)
    anyw = pl.BlockSpec(memory_space=pl.ANY)
    shape = jax.ShapeDtypeStruct
    dma = pltpu.SemaphoreType.DMA
    tok, pg, dec_low, dec_high, loss = pl.pallas_call(
        functools.partial(exchange_kernel, n, group, (PLAN_END, PLAN_MID)),
        out_shape=(
            shape((n, rows, width), BF16),
            shape((n, rows, latents), BF16),
            shape((latents, width // 2), BF16),
            shape((latents, width // 2), BF16),
            shape((8, 128), F32),
        ),
        in_specs=[vmem, anyw, vmem, anyw, vmem, anyw],
        out_specs=(anyw, anyw, anyw, anyw, vmem),
        scratch_shapes=[
            pltpu.VMEM((width, latents), BF16),
            pltpu.VMEM((latents, width), BF16),
            pltpu.VMEM((n, rows, latents), jnp.int32),
            pltpu.VMEM((n, rows, width), BF16),
            pltpu.VMEM((groups, 2, span // 2, latents), F32),
            pltpu.VMEM((groups, 2, span // 2, latents), F32),
            pltpu.VMEM((n, rows, latents), BF16),
            pltpu.VMEM((n, rows, width), BF16),
            pltpu.VMEM((n, rows, width), BF16),
            pltpu.VMEM((2, groups, rows // 2, width), BF16),
            pltpu.VMEM((groups, rows, width), BF16),
            pltpu.VMEM((groups, rows, width), BF16),
            pltpu.VMEM((n, rows, width), BF16),
            pltpu.VMEM((groups, span, latents), F32),
            pltpu.VMEM((groups, span, latents), F32),
            pltpu.VMEM((n, rows, latents), BF16),
            pltpu.VMEM((8, latents), F32),
            pltpu.VMEM((8, latents), F32),
            pltpu.VMEM((8, latents), F32),
            pltpu.VMEM((latents, 128), F32),
            pltpu.VMEM((latents, width), F32),
            pltpu.VMEM((latents, width), BF16),
            pltpu.VMEM((11, 8, 128), F32),
            dma((3,)), dma((1 + groups + width // min(512, width),)),
            dma, dma, dma((n, 2)), dma((n, 2)), dma((2, groups)), dma((2, groups)), dma((2,)),
            dma((groups, 2)), dma, dma, dma((6,)), dma((11,)),
        ],
        compiler_params=pltpu.CompilerParams(
            collective_id=0, has_side_effects=True, vmem_limit_bytes=45 << 20),
    )(activations[0], enc_weight[0], enc_bias[None], decoder, dec_bias,
      active_mask.reshape(n, rows, latents))
    grad_enc, grad_dec, loss = pl.pallas_call(
        grads_kernel,
        out_shape=(
            shape((width, latents), BF16),
            shape((latents, width), BF16),
            shape((1, 1), F32),
        ),
        in_specs=[vmem, vmem, anyw, anyw, vmem],
        out_specs=(anyw, anyw, vmem),
        scratch_shapes=[pltpu.VMEM((width, latents), BF16), dma((2 + width // min(512, width),))],
        compiler_params=pltpu.CompilerParams(vmem_limit_bytes=12 << 20),
    )(tok.reshape(tokens, width), pg.reshape(tokens, latents), dec_low, dec_high, loss)
    return (grad_enc[None], grad_dec[None], loss.reshape(()))


def solution(mesh):
    placed = (
        P("layer", "latent", None),
        P("layer", None, "latent"),
        P("latent"),
        P("layer", "latent", None),
        P("layer", None),
        P(None, "latent"),
    )
    n = mesh.shape["latent"]

    def per_device(activations, *others):
        rows = activations.shape[1]
        if rows == 32 and n == 16:
            return fast_step(n, activations, *others)
        return plain_step(activations, *others)

    return jax.shard_map(
        per_device,
        mesh=mesh,
        in_specs=placed,
        out_specs=(P("layer", None, "latent"), P("layer", "latent", None), P()),
        check_vma=False,
    )
```

```python
import functools

import jax
import jax.numpy as jnp
from jax import lax
from jax.experimental import pallas as pl
from jax.experimental.pallas import tpu as pltpu
from jax.sharding import PartitionSpec as P

sparsity_weight = 0.4
MESH = pl.DeviceIdType.MESH
F32 = jnp.float32
BF16 = jnp.bfloat16


PLAN_END = (
    "r00", "c10", "r01", "d00", "c11", "c20", "E01", "d01", "c30", "E00", "C01", "E10",
    "c31", "r30", "E11", "c21", "r31", "C10", "E20", "C11", "C20", "E30", "E21", "F10",
    "C30", "F20", "C21", "F11", "C00", "E31", "U20", "F30", "C31", "U10", "U11", "F21",
    "U30", "F31", "F00", "U21", "U31", "F01", "X0", "R00", "X1", "K10", "R01", "K11",
    "D00", "K20", "D01", "K21", "G0", "K30", "V0", "H0", "K31", "G1", "R30", "V1",
    "R31", "G2", "V2", "H1", "H2", "G3", "V3", "H3",
)
PLAN_MID = (
    "c00", "r10", "r11", "c20", "c01", "c30", "d10", "c31", "d11", "E01", "E00", "C01",
    "E10", "c21", "E11", "r30", "d20", "r31", "C10", "E20", "C11", "d21", "C20", "E30",
    "E21", "C30", "F00", "F20", "C21", "C00", "F30", "E31", "F21", "C31", "U20", "U30",
    "F01", "U21", "F31", "F11", "F10", "U00", "U01", "U31", "X0", "R10", "X1", "K00",
    "D10", "K20", "R11", "K21", "K01", "K30", "D11", "G0", "K31", "V0", "D21", "R30",
    "H0", "D20", "G1", "R31", "V1", "G2", "V2", "H1", "H2", "G3", "V3", "H3",
)
ORDERS = ((0, 1, 2, 3), (1, 0, 2, 3))
CORNER_UP = ({0: (1,)}, {1: (1, -1), 2: (-1,)})


def plain_step(activations, enc_weight, enc_bias, dec_weight, dec_bias, active_mask):
    local_rows = activations[0]
    encoder = enc_weight[0]
    decoder = dec_weight[0]
    token_all = lax.all_gather(local_rows, "latent", axis=0, tiled=True)
    layer_pre = jnp.dot(token_all, encoder, preferred_element_type=jnp.float32)
    dec_float = decoder.astype(jnp.float32)
    row_norm = jnp.sqrt(jnp.sum(dec_float * dec_float, axis=1) + 1e-06)
    preact, norm_sum = lax.psum((layer_pre, row_norm), "layer")
    preact = preact + enc_bias
    gating = active_mask.astype(jnp.float32)
    latent_code = preact * gating
    code_b = latent_code.astype(jnp.bfloat16)
    layer_index = lax.axis_index("layer")
    recon_share = (
        lax.psum_scatter(
            jnp.dot(code_b, decoder, preferred_element_type=jnp.float32),
            "latent",
            scatter_dimension=0,
            tiled=True,
        )
        + dec_bias[0]
    )
    error_share = recon_share - local_rows.astype(jnp.float32)
    square_part = 0.5 * jnp.sum(error_share * error_share)
    error_b = lax.all_gather(error_share.astype(jnp.bfloat16), "latent", axis=0, tiled=True)
    layer_grad = jnp.einsum("td,fd->tf", error_b, decoder, preferred_element_type=jnp.float32)
    code_grad = lax.psum(layer_grad, "layer") + sparsity_weight * norm_sum
    preact_grad = (code_grad * gating).astype(jnp.bfloat16)
    grad_enc = jnp.einsum(
        "td,tf->df", token_all, preact_grad, preferred_element_type=jnp.float32
    ).astype(jnp.bfloat16)
    code_total = jnp.sum(latent_code, axis=0)
    shrink = sparsity_weight * code_total[:, None] * dec_float / row_norm[:, None]
    grad_dec = (
        jnp.einsum("tf,td->fd", code_b, error_b, preferred_element_type=jnp.float32) + shrink
    ).astype(jnp.bfloat16)
    sparse_part = jnp.where(
        layer_index == 0, sparsity_weight * jnp.sum(latent_code * norm_sum), 0.0
    )
    loss_total = lax.psum(square_part + sparse_part, ("layer", "latent"))
    loss_value = loss_total / (active_mask.shape[0] * token_all.shape[1])
    return (grad_enc[None], grad_dec[None], loss_value)


def exchange_kernel(n, group, plans, act_hbm, enc_hbm, bias_hbm, dec_hbm, dbias_hbm, mask_hbm,
                    tok_out, pg_out, dec_low, dec_high, loss_out,
                    enc, dec, mask, tok, pre_own, pre_recv, code,
                    rs_send, rs_recv, rs_half, up_send, up_recv, err, lg_own, lg_recv, dec_t, pg,
                    norm_own, norm_recv, total, coef, acc, loss_all, act, bias, dbias,
                    load_sem, out_sem,
                    gather_sem, sum_sem, ag_r, er_r, rs_r, rs_hr, up_r,
                    pair_r, nm_s, nm_r, ls_s, ls_r):
    me = lax.axis_index("latent")
    layer = lax.axis_index("layer")
    other = 1 - layer
    rows, width = act.shape
    latents = mask.shape[2]
    tokens = n * rows
    span = group * rows
    groups = n // group
    mine = me // group
    spot = lax.rem(me, group)
    low = mine < groups // 2
    at_end = (mine == 0) | (mine == groups - 1)
    toward = jnp.where(low, 1, -1)

    def plane(q):
        return jnp.where(low, q, groups - 1 - q)

    def place(step):
        return plane(jnp.where(at_end, ORDERS[0][step], ORDERS[1][step]))

    side_x = spot ^ 1
    side_y = spot ^ 2
    corner = spot ^ 3
    sides = (side_x, side_y)
    half_rows = rows // 2
    half_span = span // 2

    def half(k):
        return pl.ds(k * half_rows, half_rows)

    def block_of(g):
        return pl.ds(g * group, group)

    loads = [
        pltpu.make_async_copy(hbm, vmem, load_sem.at[i])
        for i, (hbm, vmem) in enumerate((
            (act_hbm, act), (dec_hbm, dec), (enc_hbm, enc), (mask_hbm, mask),
            (bias_hbm, bias), (dbias_hbm, dbias)))
    ]
    for load in loads:
        load.start()

    barrier = pltpu.get_barrier_semaphore()
    others = [lax.rem(mine + k, groups) * group + spot for k in range(1, groups)]
    partners = [mine * group + side_x, mine * group + side_y] + others
    for partner in partners:
        pl.semaphore_signal(barrier, inc=1, device_id={"latent": partner}, device_id_type=MESH)
    pl.semaphore_signal(barrier, inc=1, device_id={"layer": other}, device_id_type=MESH)
    pl.semaphore_wait(barrier, len(partners) + 1)

    def latent_copy(src, dst, send, recv, target):
        return pltpu.make_async_remote_copy(
            src_ref=src, dst_ref=dst, send_sem=send, recv_sem=recv,
            device_id={"latent": target}, device_id_type=MESH)

    def layer_copy(src, dst, send, recv):
        return pltpu.make_async_remote_copy(
            src_ref=src, dst_ref=dst, send_sem=send, recv_sem=recv,
            device_id={"layer": other}, device_id_type=MESH)

    class Gather:
        def __init__(self, buf, first, recv_sem):
            self.buf, self.first, self.recv_sem = buf, first, recv_sem
            self.started = [0, 0]
            self.seen = (set(), set())

        def piece(self, q, where, k):
            return self.buf.at[plane(q) * group + where, half(k)]

        def wait(self, role, q, where, k, key):
            if (key, q, k) in self.seen[role]:
                return
            self.seen[role].add((key, q, k))
            part = self.piece(q, where, k)
            latent_copy(
                part, part, gather_sem,
                self.recv_sem.at[plane(q) * group + where, k], me).wait_recv()

        def send(self, role, q, where, k, target, own=False):
            part = self.piece(q, where, k)
            latent_copy(
                self.first.at[half(k)] if own else part, part, gather_sem,
                self.recv_sem.at[plane(q) * group + where, k], target()).start()
            self.started[role] += 1

        def along(self, role, q, where, k, shift, own=False):
            self.send(role, q, where, k, lambda: me + shift * toward * group, own)

        def across(self, role, q, k, own=False):
            for to in sides:
                self.send(role, q, spot, k, lambda to=to: mine * group + to, own)

        def run(self, role, event, q, k):
            if event == "o":
                self.across(role, q, k, own=True)
                for shift in ((1,), (1, -1))[role]:
                    self.along(role, q, spot, k, shift, own=True)
            elif event == "c":
                self.wait(role, q, spot, k, "s")
                if role == 1:
                    self.along(role, q, spot, k, 1 if q == 0 else -1)
                self.across(role, q, k)
            elif event == "r":
                self.wait(role, q, sides[k], k, "xy"[k])
                self.send(role, q, sides[k], k, lambda: mine * group + sides[1 - k])
            else:
                self.wait(role, q, corner, k, "d")
                for shift in CORNER_UP[role].get(q, ()):
                    self.along(role, q, corner, k, shift)

        def settle(self, role, q, k):
            if q != role:
                self.wait(role, q, spot, k, "s")
            self.wait(role, q, side_x, k, "x")
            self.wait(role, q, side_y, k, "y")
            self.wait(role, q, corner, k, "d")

    tokens_in = Gather(tok, act, ag_r)
    errors_in = Gather(err, err.at[me], er_r)

    def by_role(do):
        @pl.when(at_end)
        def _():
            do(0)

        @pl.when(jnp.logical_not(at_end))
        def _():
            do(1)

    def pre_copy(g, k):
        return layer_copy(pre_own.at[g, k], pre_recv.at[g, k], sum_sem, pair_r.at[g, k])

    def lg_copy(g):
        return layer_copy(lg_own.at[g], lg_recv.at[g], sum_sem, pair_r.at[g, 0])

    def corner_copy(g, k):
        return latent_copy(
            rs_send.at[g * group + corner, half(k)], rs_half.at[k, g],
            sum_sem, rs_hr.at[k, g], mine * group + sides[1 - k])

    def side_copy(g, i, k):
        return latent_copy(
            rs_send.at[g * group + sides[i], half(k)], rs_recv.at[g * group + spot, half(k)],
            sum_sem, rs_r.at[k, g], mine * group + sides[i])

    def pieces(count):
        return acc.at[pl.ds(0, count * half_rows // 2)]

    def side_arrived(g, k):
        part = pieces(2)
        latent_copy(part, part, sum_sem, rs_r.at[k, g], me).wait_recv()

    def up_copy(g, k):
        return latent_copy(
            up_send.at[g, half(k)], up_recv.at[mine, half(k)],
            sum_sem, up_r.at[k], g * group + spot)

    def up_arrived(k):
        part = pieces(groups - 1)
        latent_copy(part, part, sum_sem, up_r.at[k], me).wait_recv()

    tile = min(512, latents)
    wide = min(512, width)
    lanes = 128

    def norm_block(block, carry):
        at = pl.multiple_of(block * lanes, lanes)
        piece = dec[pl.ds(at, lanes), :].astype(F32)
        dec_t[:, pl.ds(at, lanes)] = dec[pl.ds(at, lanes), :].T
        sums = jnp.sum(piece * piece, axis=1, keepdims=True)
        norm = jnp.sqrt(sums + 1e-06)
        norm_own[:, pl.ds(at, lanes)] = jnp.broadcast_to(norm, (lanes, lanes)).T[0:8, :]
        return carry

    norm_copy = layer_copy(norm_own, norm_recv, nm_s, nm_r)

    def encode(step, k):
        g = place(step)
        left = tok[block_of(g), half(k)].reshape(half_span, width)
        for c in range(latents // tile):
            cols = pl.ds(c * tile, tile)
            pre_own[g, k, :, cols] = jnp.dot(left, enc[:, cols], preferred_element_type=F32)
        pre_copy(g, k).start()

    def decode(step, k):
        g = place(step)
        pre_copy(g, k).wait_recv()
        for c in range(latents // tile):
            cols = pl.ds(c * tile, tile)
            gating = mask[block_of(g), half(k), cols].reshape(half_span, tile).astype(F32)
            preact = pre_own[g, k, :, cols] + pre_recv[g, k, :, cols] + bias[0:1, cols]
            latent = preact * gating
            total[0:1, cols] += jnp.sum(latent, axis=0, keepdims=True)
            code[block_of(g), half(k), cols] = latent.astype(BF16).reshape(group, half_rows, tile)
        left = code[block_of(g), half(k)].reshape(half_span, latents)
        for c in range(width // wide):
            cols = pl.ds(c * wide, wide)
            part = jnp.dot(left, dec[:, cols], preferred_element_type=F32).astype(BF16)
            rs_send[block_of(g), half(k), cols] = part.reshape(group, half_rows, wide)
        corner_copy(g, k).start()
        side_copy(g, 1 - k, k).start()

    def fold(q, k):
        g = plane(q)
        part = rs_half.at[k, g]
        latent_copy(part, part, sum_sem, rs_hr.at[k, g], me).wait_recv()
        at = (g * group + sides[k], half(k))
        rs_send[at] = (rs_send[at].astype(F32) + rs_half[k, g].astype(F32)).astype(BF16)
        side_copy(g, k, k).start()

    def plane_sum(g, k, cols):
        part = rs_send[g * group + spot, half(k), cols].astype(F32)
        for source in sides:
            part = part + rs_recv[g * group + source, half(k), cols].astype(F32)
        return part

    def climb(q, k):
        g = plane(q)
        side_arrived(g, k)
        for c in range(width // wide):
            cols = pl.ds(c * wide, wide)
            up_send[g, half(k), cols] = plane_sum(g, k, cols).astype(BF16)
        up_copy(g, k).start()

    squares = []

    def error(k):
        side_arrived(mine, k)
        planes = [lax.rem(mine + j, groups) for j in range(1, groups)]
        up_arrived(k)
        for c in range(width // wide):
            cols = pl.ds(c * wide, wide)
            recon = plane_sum(mine, k, cols)
            for g in planes:
                recon = recon + up_recv[g, half(k), cols].astype(F32)
            gap = recon + dbias[0:1, cols] - act[half(k), cols].astype(F32)
            squares.append(jnp.sum(gap * gap))
            err[me, half(k), cols] = gap.astype(BF16)
        by_role(lambda role: errors_in.run(role, "o", role, k))
        if len(squares) == 2 * (width // wide):
            settle_sums()

    def loss_copy(index, source, slot, target):
        return latent_copy(
            loss_all.at[source], loss_all.at[slot], ls_s.at[index], ls_r.at[slot], target)

    def loss_z(j):
        return loss_copy(j + 1, 4, 5 + mine, others[j - 1])

    def loss_pair():
        return layer_copy(loss_all.at[9], loss_all.at[10], ls_s.at[5], ls_r.at[10])

    def settle_sums():
        tok_copy.start()
        norm_copy.wait()
        norm_sum = norm_own[0:1, :] + norm_recv[0:1, :]
        sparse = sparsity_weight * jnp.sum(total[0:1, :] * norm_sum)
        ratio = sparsity_weight * total[0:1, :] / norm_own[0:1, :]
        coef[...] = jnp.broadcast_to(ratio, (lanes, latents)).T
        norm_recv[...] = jnp.broadcast_to(sparsity_weight * norm_sum, norm_recv.shape)
        partial = 0.5 * sum(squares) + jnp.where(layer == 0, sparse, 0.0)
        loss_all[0] = jnp.broadcast_to(partial, loss_all.shape[1:])
        loss_copy(0, 0, 1, partners[0]).start()

    def loss_step(step):
        if step == 0:
            loss_copy(0, 0, 1, partners[0]).wait()
            loss_all[2] = loss_all[0] + loss_all[1]
            loss_copy(1, 2, 3, partners[1]).start()
        elif step == 1:
            loss_copy(1, 2, 3, partners[1]).wait()
            loss_all[4] = loss_all[2] + loss_all[3]
            loss_all[5 + mine] = loss_all[4]
            for j in range(1, groups):
                loss_z(j).start()
        elif step == 2:
            for j in range(1, groups):
                latent_copy(
                    loss_all.at[4], loss_all.at[5 + lax.rem(mine + j, groups)],
                    ls_s.at[j + 1], ls_r.at[5 + lax.rem(mine + j, groups)], me).wait_recv()
                loss_z(j).wait_send()
            loss_all[9] = loss_all[5] + loss_all[6] + loss_all[7] + loss_all[8]
            loss_pair().start()
        else:
            loss_pair().wait()
            loss_out[...] = (loss_all[9] + loss_all[10]) / (tokens * width)

    def grad(step, k):
        g = place(step)
        left = err[block_of(g)].reshape(span, width)
        for c in range(latents // tile):
            cols = pl.ds(c * tile, tile)
            lg_own[g, :, cols] = jnp.dot(left, dec_t[:, cols], preferred_element_type=F32)
        lg_copy(g).start()
        loss_step(step)

    def gate(step, k):
        g = place(step)
        lg_copy(g).wait_recv()
        for c in range(latents // tile):
            cols = pl.ds(c * tile, tile)
            gating = mask[block_of(g), :, cols].reshape(span, tile).astype(F32)
            code_grad = lg_own[g, :, cols] + lg_recv[g, :, cols] + norm_recv[0:1, cols]
            pg[block_of(g), :, cols] = (code_grad * gating).astype(BF16).reshape(group, rows, tile)
        pg_copy(g).start()

    def pg_copy(g):
        return pltpu.make_async_copy(pg.at[block_of(g)], pg_out.at[block_of(g)], out_sem.at[1 + g])

    def dec_copy(c):
        cols = pl.ds(c * wide, wide)
        part = width // 2
        out = (dec_low, dec_high)[c * wide // part]
        return pltpu.make_async_copy(
            dec.at[:, cols], out.at[:, pl.ds(c * wide % part, wide)], out_sem.at[1 + groups + c])

    def outer(step, k):
        g = place(step)
        left = code[block_of(g)].reshape(span, latents)
        right = err[block_of(g)].reshape(span, width)
        for c in range(width // wide):
            cols = pl.ds(c * wide, wide)
            part = lax.dot_general(
                left, right[:, c * wide:(c + 1) * wide], (((0,), (0,)), ((), ())),
                preferred_element_type=F32)
            if step == 0:
                acc[:, cols] = part + coef[:, 0:1] * dec[:, cols].astype(F32)
            elif step < groups - 1:
                acc[:, cols] += part
            else:
                dec[:, cols] = (acc[:, cols] + part).astype(BF16)
                dec_copy(c).start()

    tok_copy = pltpu.make_async_copy(tok, tok_out, out_sem.at[0])

    def open_tokens(k):
        by_role(lambda role: tokens_in.run(role, "o", role, k))

    loads[0].wait()
    for k in range(2):
        open_tokens(k)
    tok[me] = act[...]
    loads[1].wait()
    lax.fori_loop(0, latents // lanes, norm_block, 0)
    norm_copy.start()
    total[...] = jnp.zeros_like(total)
    for load in loads[2:]:
        load.wait()

    steps = {"E": encode, "C": decode, "X": error, "G": grad, "V": outer, "H": gate}
    taken = [0, 0]

    def between(role, token):
        plan = plans[role]
        while taken[role] < len(plan) and plan[taken[role]][0] not in steps:
            event = plan[taken[role]]
            q, k = int(event[1]), int(event[2])
            if event[0] == "F":
                fold(q, k)
            elif event[0] == "U":
                climb(q, k)
            elif event[0] in "crd":
                tokens_in.run(role, event[0], q, k)
            else:
                errors_in.run(role, event[0].lower().replace("k", "c"), q, k)
            taken[role] += 1
        taken[role] += 1
        if token and token[0] == "E":
            tokens_in.settle(role, ORDERS[role][int(token[1])], int(token[2]))
        elif token and token[0] in "GV":
            for k in range(2):
                errors_in.settle(role, ORDERS[role][int(token[1])], k)

    for token in [token for token in plans[0] if token[0] in steps] + [""]:
        by_role(lambda role: between(role, token))
        if token and token[0] == "X":
            error(int(token[1]))
        elif token:
            steps[token[0]](int(token[1]), int(token[2]) if len(token) > 2 else 0)

    def sent(sem, count):
        part = pieces(count)
        latent_copy(part, part, sem, sem, me).wait_send()

    by_role(lambda role: sent(gather_sem, tokens_in.started[role] + errors_in.started[role]))
    pairs = 2 * groups * span * latents * 4 // (half_rows * width * 2)
    sent(sum_sem, 6 * groups + 2 * (groups - 1) + pairs)

    def finish_group(g, carry):
        pg_copy(g).wait()
        return carry

    lax.fori_loop(0, groups, finish_group, 0)
    for c in range(width // wide):
        dec_copy(c).wait()
    tok_copy.wait()


def grads_kernel(tok, pg, dec_low, dec_high, loss, enc_out, dec_out, loss_out, buf, sem):
    part = dec_low.shape[1]
    copies = [
        pltpu.make_async_copy(half, dec_out.at[:, pl.ds(i * part, part)], sem.at[i])
        for i, half in enumerate((dec_low, dec_high))
    ]
    for copy in copies:
        copy.start()
    loss_out[...] = loss[0:1, 0:1]
    width = tok.shape[1]
    tile = min(512, width)
    for i in range(width // tile):
        here = pl.ds(i * tile, tile)
        buf[here, :] = lax.dot_general(
            tok[:, here], pg[...], (((0,), (0,)), ((), ())), preferred_element_type=F32).astype(BF16)
        copies.append(pltpu.make_async_copy(buf.at[here], enc_out.at[here], sem.at[2 + i]))
        copies[-1].start()
    for copy in copies:
        copy.wait()


def fast_step(n, activations, enc_weight, enc_bias, dec_weight, dec_bias, active_mask):
    rows, width = activations.shape[1:]
    tokens, latents = active_mask.shape
    group = 4
    groups = n // group
    span = group * rows
    decoder = dec_weight[0]
    vmem = pl.BlockSpec(memory_space=pltpu.VMEM)
    anyw = pl.BlockSpec(memory_space=pl.ANY)
    shape = jax.ShapeDtypeStruct
    dma = pltpu.SemaphoreType.DMA
    def keep(x):
        return pltpu.with_memory_space_constraint(x, pltpu.HBM)

    tok, pg, dec_low, dec_high, loss = pl.pallas_call(
        functools.partial(exchange_kernel, n, group, (PLAN_END, PLAN_MID)),
        out_shape=(
            shape((n, rows, width), BF16),
            shape((n, rows, latents), BF16),
            shape((latents, width // 2), BF16),
            shape((latents, width // 2), BF16),
            shape((8, 128), F32),
        ),
        in_specs=[anyw] * 6,
        out_specs=(anyw, anyw, anyw, anyw, vmem),
        scratch_shapes=[
            pltpu.VMEM((width, latents), BF16),
            pltpu.VMEM((latents, width), BF16),
            pltpu.VMEM((n, rows, latents), jnp.int32),
            pltpu.VMEM((n, rows, width), BF16),
            pltpu.VMEM((groups, 2, span // 2, latents), F32),
            pltpu.VMEM((groups, 2, span // 2, latents), F32),
            pltpu.VMEM((n, rows, latents), BF16),
            pltpu.VMEM((n, rows, width), BF16),
            pltpu.VMEM((n, rows, width), BF16),
            pltpu.VMEM((2, groups, rows // 2, width), BF16),
            pltpu.VMEM((groups, rows, width), BF16),
            pltpu.VMEM((groups, rows, width), BF16),
            pltpu.VMEM((n, rows, width), BF16),
            pltpu.VMEM((groups, span, latents), F32),
            pltpu.VMEM((groups, span, latents), F32),
            pltpu.VMEM((width, latents), BF16),
            pltpu.VMEM((n, rows, latents), BF16),
            pltpu.VMEM((8, latents), F32),
            pltpu.VMEM((8, latents), F32),
            pltpu.VMEM((8, latents), F32),
            pltpu.VMEM((latents, 128), F32),
            pltpu.VMEM((latents, width), F32),
            pltpu.VMEM((11, 8, 128), F32),
            pltpu.VMEM((rows, width), BF16),
            pltpu.VMEM((1, latents), F32),
            pltpu.VMEM((1, width), F32),
            dma((6,)), dma((1 + groups + width // min(512, width),)),
            dma, dma, dma((n, 2)), dma((n, 2)), dma((2, groups)), dma((2, groups)), dma((2,)),
            dma((groups, 2)), dma, dma, dma((6,)), dma((11,)),
        ],
        compiler_params=pltpu.CompilerParams(
            collective_id=0, has_side_effects=True, vmem_limit_bytes=45 << 20),
    )(keep(activations[0]), enc_weight[0], keep(enc_bias[None]), decoder, keep(dec_bias),
      active_mask.reshape(n, rows, latents))
    grad_enc, grad_dec, loss = pl.pallas_call(
        grads_kernel,
        out_shape=(
            shape((width, latents), BF16),
            shape((latents, width), BF16),
            shape((1, 1), F32),
        ),
        in_specs=[vmem, vmem, anyw, anyw, vmem],
        out_specs=(anyw, anyw, vmem),
        scratch_shapes=[pltpu.VMEM((width, latents), BF16), dma((2 + width // min(512, width),))],
        compiler_params=pltpu.CompilerParams(vmem_limit_bytes=12 << 20),
    )(tok.reshape(tokens, width), pg.reshape(tokens, latents), dec_low, dec_high, loss)
    return (grad_enc[None], grad_dec[None], loss.reshape(()))


def solution(mesh):
    placed = (
        P("layer", "latent", None),
        P("layer", None, "latent"),
        P("latent"),
        P("layer", "latent", None),
        P("layer", None),
        P(None, "latent"),
    )
    n = mesh.shape["latent"]

    def per_device(activations, *others):
        rows = activations.shape[1]
        if rows == 32 and n == 16:
            return fast_step(n, activations, *others)
        return plain_step(activations, *others)

    return jax.shard_map(
        per_device,
        mesh=mesh,
        in_specs=placed,
        out_specs=(P("layer", None, "latent"), P("layer", "latent", None), P()),
        check_vma=False,
    )
```

```python
import functools

import jax
import jax.numpy as jnp
from jax import lax
from jax.experimental import pallas as pl
from jax.experimental.pallas import tpu as pltpu
from jax.sharding import PartitionSpec as P

sparsity_weight = 0.4
MESH = pl.DeviceIdType.MESH
F32 = jnp.float32
BF16 = jnp.bfloat16


PLAN_END = (
    "r00", "c10", "r01", "d00", "c11", "c20", "E01", "d01", "c30", "E00", "C01", "E10",
    "c31", "r30", "E11", "c21", "r31", "C10", "E20", "C11", "C20", "E30", "E21", "F10",
    "C30", "F20", "C21", "F11", "C00", "E31", "U20", "F30", "C31", "U10", "U11", "F21",
    "U30", "F31", "F00", "U21", "U31", "F01", "X0", "R00", "X1", "K10", "R01", "K11",
    "D00", "K20", "D01", "K21", "K31", "G0", "K30", "H0", "G1", "R30", "R31", "V1",
    "G2", "G3", "H1", "H2", "V3", "H3",
)
PLAN_MID = (
    "c00", "r10", "r11", "c20", "c01", "c30", "d10", "c31", "d11", "E01", "E00", "C01",
    "E10", "c21", "E11", "r30", "d20", "r31", "C10", "E20", "C11", "d21", "C20", "E30",
    "E21", "C30", "F00", "F20", "C21", "C00", "F30", "E31", "F21", "C31", "U20", "U30",
    "F01", "U21", "F31", "F11", "F10", "U00", "U01", "U31", "X0", "R10", "X1", "K00",
    "D10", "K20", "R11", "K21", "K01", "K30", "D11", "G0", "K31", "D21", "R30", "H0",
    "D20", "G1", "R31", "V1", "G2", "G3", "H1", "H2", "V3", "H3",
)
ORDERS = ((0, 1, 2, 3), (1, 0, 2, 3))
CORNER_UP = ({0: (1,)}, {1: (1, -1), 2: (-1,)})


def plain_step(activations, enc_weight, enc_bias, dec_weight, dec_bias, active_mask):
    local_rows = activations[0]
    encoder = enc_weight[0]
    decoder = dec_weight[0]
    token_all = lax.all_gather(local_rows, "latent", axis=0, tiled=True)
    layer_pre = jnp.dot(token_all, encoder, preferred_element_type=jnp.float32)
    dec_float = decoder.astype(jnp.float32)
    row_norm = jnp.sqrt(jnp.sum(dec_float * dec_float, axis=1) + 1e-06)
    preact, norm_sum = lax.psum((layer_pre, row_norm), "layer")
    preact = preact + enc_bias
    gating = active_mask.astype(jnp.float32)
    latent_code = preact * gating
    code_b = latent_code.astype(jnp.bfloat16)
    layer_index = lax.axis_index("layer")
    recon_share = (
        lax.psum_scatter(
            jnp.dot(code_b, decoder, preferred_element_type=jnp.float32),
            "latent",
            scatter_dimension=0,
            tiled=True,
        )
        + dec_bias[0]
    )
    error_share = recon_share - local_rows.astype(jnp.float32)
    square_part = 0.5 * jnp.sum(error_share * error_share)
    error_b = lax.all_gather(error_share.astype(jnp.bfloat16), "latent", axis=0, tiled=True)
    layer_grad = jnp.einsum("td,fd->tf", error_b, decoder, preferred_element_type=jnp.float32)
    code_grad = lax.psum(layer_grad, "layer") + sparsity_weight * norm_sum
    preact_grad = (code_grad * gating).astype(jnp.bfloat16)
    grad_enc = jnp.einsum(
        "td,tf->df", token_all, preact_grad, preferred_element_type=jnp.float32
    ).astype(jnp.bfloat16)
    code_total = jnp.sum(latent_code, axis=0)
    shrink = sparsity_weight * code_total[:, None] * dec_float / row_norm[:, None]
    grad_dec = (
        jnp.einsum("tf,td->fd", code_b, error_b, preferred_element_type=jnp.float32) + shrink
    ).astype(jnp.bfloat16)
    sparse_part = jnp.where(
        layer_index == 0, sparsity_weight * jnp.sum(latent_code * norm_sum), 0.0
    )
    loss_total = lax.psum(square_part + sparse_part, ("layer", "latent"))
    loss_value = loss_total / (active_mask.shape[0] * token_all.shape[1])
    return (grad_enc[None], grad_dec[None], loss_value)


def exchange_kernel(n, group, plans, act_hbm, enc_hbm, bias_hbm, dec_hbm, dbias_hbm, mask_hbm,
                    tok_out, pg_out, dec_low, dec_high, loss_out,
                    enc, dec, mask, tok, pre_own, pre_recv, code,
                    rs_send, rs_recv, rs_half, up_send, up_recv, err, lg_own, lg_recv, dec_t, pg,
                    norm_own, norm_recv, total, coef, acc, loss_all, act, bias, dbias,
                    load_sem, out_sem,
                    gather_sem, sum_sem, ag_r, er_r, rs_r, rs_hr, up_r,
                    pair_r, nm_s, nm_r, ls_s, ls_r):
    me = lax.axis_index("latent")
    layer = lax.axis_index("layer")
    other = 1 - layer
    rows, width = act.shape
    latents = mask.shape[2]
    tokens = n * rows
    span = group * rows
    groups = n // group
    mine = me // group
    spot = lax.rem(me, group)
    low = mine < groups // 2
    at_end = (mine == 0) | (mine == groups - 1)
    toward = jnp.where(low, 1, -1)

    def plane(q):
        return jnp.where(low, q, groups - 1 - q)

    def place(step):
        return plane(jnp.where(at_end, ORDERS[0][step], ORDERS[1][step]))

    side_x = spot ^ 1
    side_y = spot ^ 2
    corner = spot ^ 3
    sides = (side_x, side_y)
    half_rows = rows // 2
    half_span = span // 2

    def half(k):
        return pl.ds(k * half_rows, half_rows)

    def block_of(g):
        return pl.ds(g * group, group)

    loads = [
        pltpu.make_async_copy(hbm, vmem, load_sem.at[i])
        for i, (hbm, vmem) in enumerate((
            (act_hbm, act), (dec_hbm, dec), (enc_hbm, enc), (mask_hbm, mask),
            (bias_hbm, bias), (dbias_hbm, dbias)))
    ]
    for load in loads:
        load.start()

    barrier = pltpu.get_barrier_semaphore()
    others = [lax.rem(mine + k, groups) * group + spot for k in range(1, groups)]
    partners = [mine * group + side_x, mine * group + side_y] + others
    for partner in partners:
        pl.semaphore_signal(barrier, inc=1, device_id={"latent": partner}, device_id_type=MESH)
    pl.semaphore_signal(barrier, inc=1, device_id={"layer": other}, device_id_type=MESH)
    pl.semaphore_wait(barrier, len(partners) + 1)

    def latent_copy(src, dst, send, recv, target):
        return pltpu.make_async_remote_copy(
            src_ref=src, dst_ref=dst, send_sem=send, recv_sem=recv,
            device_id={"latent": target}, device_id_type=MESH)

    def layer_copy(src, dst, send, recv):
        return pltpu.make_async_remote_copy(
            src_ref=src, dst_ref=dst, send_sem=send, recv_sem=recv,
            device_id={"layer": other}, device_id_type=MESH)

    class Gather:
        def __init__(self, buf, first, recv_sem, far):
            self.buf, self.first, self.recv_sem, self.far = buf, first, recv_sem, far
            self.started = [0, 0]
            self.seen = (set(), set())

        def piece(self, q, where, k):
            return self.buf.at[plane(q) * group + where, half(k)]

        def wait(self, role, q, where, k, key):
            if (key, q, k) in self.seen[role]:
                return
            self.seen[role].add((key, q, k))
            part = self.piece(q, where, k)
            latent_copy(
                part, part, gather_sem,
                self.recv_sem.at[plane(q) * group + where, k], me).wait_recv()

        def send(self, role, q, where, k, target, own=False):
            part = self.piece(q, where, k)
            latent_copy(
                self.first.at[half(k)] if own else part, part, gather_sem,
                self.recv_sem.at[plane(q) * group + where, k], target()).start()
            self.started[role] += 1

        def along(self, role, q, where, k, shift, own=False):
            self.send(role, q, where, k, lambda: me + shift * toward * group, own)

        def across(self, role, q, k, own=False):
            for to in sides:
                self.send(role, q, spot, k, lambda to=to: mine * group + to, own)

        def run(self, role, event, q, k):
            if event == "o":
                self.across(role, q, k, own=True)
                for shift in ((1, groups - 1) if self.far[k] else (1,), (1, -1))[role]:
                    self.along(role, q, spot, k, shift, own=True)
            elif event == "c":
                self.wait(role, q, spot, k, "s")
                if role == 1 and not (q == groups - 1 and self.far[k]):
                    self.along(role, q, spot, k, 1 if q == 0 else -1)
                self.across(role, q, k)
            elif event == "r":
                self.wait(role, q, sides[k], k, "xy"[k])
                self.send(role, q, sides[k], k, lambda: mine * group + sides[1 - k])
            else:
                self.wait(role, q, corner, k, "d")
                for shift in CORNER_UP[role].get(q, ()):
                    self.along(role, q, corner, k, shift)

        def settle(self, role, q, k):
            if q != role:
                self.wait(role, q, spot, k, "s")
            self.wait(role, q, side_x, k, "x")
            self.wait(role, q, side_y, k, "y")
            self.wait(role, q, corner, k, "d")

    tokens_in = Gather(tok, act, ag_r, (False, False))
    errors_in = Gather(err, err.at[me], er_r, (False, True))

    def by_role(do):
        @pl.when(at_end)
        def _():
            do(0)

        @pl.when(jnp.logical_not(at_end))
        def _():
            do(1)

    def pre_copy(g, k):
        return layer_copy(pre_own.at[g, k], pre_recv.at[g, k], sum_sem, pair_r.at[g, k])

    def lg_copy(g):
        return layer_copy(lg_own.at[g], lg_recv.at[g], sum_sem, pair_r.at[g, 0])

    def corner_copy(g, k):
        return latent_copy(
            rs_send.at[g * group + corner, half(k)], rs_half.at[k, g],
            sum_sem, rs_hr.at[k, g], mine * group + sides[1 - k])

    def side_copy(g, i, k):
        return latent_copy(
            rs_send.at[g * group + sides[i], half(k)], rs_recv.at[g * group + spot, half(k)],
            sum_sem, rs_r.at[k, g], mine * group + sides[i])

    def pieces(count):
        return acc.at[pl.ds(0, count * half_rows // 2)]

    def side_arrived(g, k):
        part = pieces(2)
        latent_copy(part, part, sum_sem, rs_r.at[k, g], me).wait_recv()

    def up_copy(g, k):
        return latent_copy(
            up_send.at[g, half(k)], up_recv.at[mine, half(k)],
            sum_sem, up_r.at[k], g * group + spot)

    def up_arrived(k):
        part = pieces(groups - 1)
        latent_copy(part, part, sum_sem, up_r.at[k], me).wait_recv()

    tile = min(512, latents)
    wide = min(512, width)
    lanes = 128

    def norm_block(block, carry):
        at = pl.multiple_of(block * lanes, lanes)
        piece = dec[pl.ds(at, lanes), :].astype(F32)
        dec_t[:, pl.ds(at, lanes)] = dec[pl.ds(at, lanes), :].T
        sums = jnp.sum(piece * piece, axis=1, keepdims=True)
        norm = jnp.sqrt(sums + 1e-06)
        norm_own[:, pl.ds(at, lanes)] = jnp.broadcast_to(norm, (lanes, lanes)).T[0:8, :]
        return carry

    norm_copy = layer_copy(norm_own, norm_recv, nm_s, nm_r)

    def encode(step, k):
        g = place(step)
        left = tok[block_of(g), half(k)].reshape(half_span, width)
        for c in range(latents // tile):
            cols = pl.ds(c * tile, tile)
            pre_own[g, k, :, cols] = jnp.dot(left, enc[:, cols], preferred_element_type=F32)
        pre_copy(g, k).start()

    def decode(step, k):
        g = place(step)
        pre_copy(g, k).wait_recv()
        for c in range(latents // tile):
            cols = pl.ds(c * tile, tile)
            gating = mask[block_of(g), half(k), cols].reshape(half_span, tile).astype(F32)
            preact = pre_own[g, k, :, cols] + pre_recv[g, k, :, cols] + bias[0:1, cols]
            latent = preact * gating
            total[0:1, cols] += jnp.sum(latent, axis=0, keepdims=True)
            code[block_of(g), half(k), cols] = latent.astype(BF16).reshape(group, half_rows, tile)
        left = code[block_of(g), half(k)].reshape(half_span, latents)
        for c in range(width // wide):
            cols = pl.ds(c * wide, wide)
            part = jnp.dot(left, dec[:, cols], preferred_element_type=F32).astype(BF16)
            rs_send[block_of(g), half(k), cols] = part.reshape(group, half_rows, wide)
        corner_copy(g, k).start()
        side_copy(g, 1 - k, k).start()

    def fold(q, k):
        g = plane(q)
        part = rs_half.at[k, g]
        latent_copy(part, part, sum_sem, rs_hr.at[k, g], me).wait_recv()
        at = (g * group + sides[k], half(k))
        rs_send[at] = (rs_send[at].astype(F32) + rs_half[k, g].astype(F32)).astype(BF16)
        side_copy(g, k, k).start()

    def plane_sum(g, k, cols):
        part = rs_send[g * group + spot, half(k), cols].astype(F32)
        for source in sides:
            part = part + rs_recv[g * group + source, half(k), cols].astype(F32)
        return part

    def climb(q, k):
        g = plane(q)
        side_arrived(g, k)
        for c in range(width // wide):
            cols = pl.ds(c * wide, wide)
            up_send[g, half(k), cols] = plane_sum(g, k, cols).astype(BF16)
        up_copy(g, k).start()

    squares = []

    def error(k):
        side_arrived(mine, k)
        planes = [lax.rem(mine + j, groups) for j in range(1, groups)]
        up_arrived(k)
        for c in range(width // wide):
            cols = pl.ds(c * wide, wide)
            recon = plane_sum(mine, k, cols)
            for g in planes:
                recon = recon + up_recv[g, half(k), cols].astype(F32)
            gap = recon + dbias[0:1, cols] - act[half(k), cols].astype(F32)
            squares.append(jnp.sum(gap * gap))
            err[me, half(k), cols] = gap.astype(BF16)
        by_role(lambda role: errors_in.run(role, "o", role, k))
        if len(squares) == 2 * (width // wide):
            settle_sums()

    def loss_copy(index, source, slot, target):
        return latent_copy(
            loss_all.at[source], loss_all.at[slot], ls_s.at[index], ls_r.at[slot], target)

    def loss_z(j):
        return loss_copy(j + 1, 4, 5 + mine, others[j - 1])

    def loss_pair():
        return layer_copy(loss_all.at[9], loss_all.at[10], ls_s.at[5], ls_r.at[10])

    def settle_sums():
        tok_copy.start()
        norm_copy.wait()
        norm_sum = norm_own[0:1, :] + norm_recv[0:1, :]
        sparse = sparsity_weight * jnp.sum(total[0:1, :] * norm_sum)
        ratio = sparsity_weight * total[0:1, :] / norm_own[0:1, :]
        coef[...] = jnp.broadcast_to(ratio, (lanes, latents)).T
        norm_recv[...] = jnp.broadcast_to(sparsity_weight * norm_sum, norm_recv.shape)
        partial = 0.5 * sum(squares) + jnp.where(layer == 0, sparse, 0.0)
        loss_all[0] = jnp.broadcast_to(partial, loss_all.shape[1:])
        loss_copy(0, 0, 1, partners[0]).start()

    def loss_step(step):
        if step == 0:
            loss_copy(0, 0, 1, partners[0]).wait()
            loss_all[2] = loss_all[0] + loss_all[1]
            loss_copy(1, 2, 3, partners[1]).start()
        elif step == 1:
            loss_copy(1, 2, 3, partners[1]).wait()
            loss_all[4] = loss_all[2] + loss_all[3]
            loss_all[5 + mine] = loss_all[4]
            for j in range(1, groups):
                loss_z(j).start()
        elif step == 2:
            for j in range(1, groups):
                latent_copy(
                    loss_all.at[4], loss_all.at[5 + lax.rem(mine + j, groups)],
                    ls_s.at[j + 1], ls_r.at[5 + lax.rem(mine + j, groups)], me).wait_recv()
                loss_z(j).wait_send()
            loss_all[9] = loss_all[5] + loss_all[6] + loss_all[7] + loss_all[8]
            loss_pair().start()
        else:
            loss_pair().wait()
            loss_out[...] = (loss_all[9] + loss_all[10]) / (tokens * width)

    def grad(step, k):
        g = place(step)
        left = err[block_of(g)].reshape(span, width)
        for c in range(latents // tile):
            cols = pl.ds(c * tile, tile)
            lg_own[g, :, cols] = jnp.dot(left, dec_t[:, cols], preferred_element_type=F32)
        lg_copy(g).start()
        loss_step(step)

    def gate(step, k):
        g = place(step)
        lg_copy(g).wait_recv()
        for c in range(latents // tile):
            cols = pl.ds(c * tile, tile)
            gating = mask[block_of(g), :, cols].reshape(span, tile).astype(F32)
            code_grad = lg_own[g, :, cols] + lg_recv[g, :, cols] + norm_recv[0:1, cols]
            pg[block_of(g), :, cols] = (code_grad * gating).astype(BF16).reshape(group, rows, tile)
        pg_copy(g).start()

    def pg_copy(g):
        return pltpu.make_async_copy(pg.at[block_of(g)], pg_out.at[block_of(g)], out_sem.at[1 + g])

    def dec_copy(c):
        cols = pl.ds(c * wide, wide)
        part = width // 2
        out = (dec_low, dec_high)[c * wide // part]
        return pltpu.make_async_copy(
            dec.at[:, cols], out.at[:, pl.ds(c * wide % part, wide)], out_sem.at[1 + groups + c])

    def outer(step, k):
        blocks = [block_of(place(step - 1)), block_of(place(step))]
        left = jnp.concatenate([code[b].reshape(span, latents) for b in blocks], axis=0)
        right = jnp.concatenate([err[b].reshape(span, width) for b in blocks], axis=0)
        for c in range(width // wide):
            cols = pl.ds(c * wide, wide)
            part = lax.dot_general(
                left, right[:, c * wide:(c + 1) * wide], (((0,), (0,)), ((), ())),
                preferred_element_type=F32)
            if step == 1:
                acc[:, cols] = part + coef[:, 0:1] * dec[:, cols].astype(F32)
            elif step < groups - 1:
                acc[:, cols] += part
            else:
                dec[:, cols] = (acc[:, cols] + part).astype(BF16)
                dec_copy(c).start()

    tok_copy = pltpu.make_async_copy(tok, tok_out, out_sem.at[0])

    def open_tokens(k):
        by_role(lambda role: tokens_in.run(role, "o", role, k))

    loads[0].wait()
    for k in range(2):
        open_tokens(k)
    tok[me] = act[...]
    loads[1].wait()
    lax.fori_loop(0, latents // lanes, norm_block, 0)
    norm_copy.start()
    total[...] = jnp.zeros_like(total)
    for load in loads[2:]:
        load.wait()

    steps = {"E": encode, "C": decode, "X": error, "G": grad, "V": outer, "H": gate}
    taken = [0, 0]

    def between(role, token):
        plan = plans[role]
        while taken[role] < len(plan) and plan[taken[role]][0] not in steps:
            event = plan[taken[role]]
            q, k = int(event[1]), int(event[2])
            if event[0] == "F":
                fold(q, k)
            elif event[0] == "U":
                climb(q, k)
            elif event[0] in "crd":
                tokens_in.run(role, event[0], q, k)
            else:
                errors_in.run(role, event[0].lower().replace("k", "c"), q, k)
            taken[role] += 1
        taken[role] += 1
        if token and token[0] == "E":
            tokens_in.settle(role, ORDERS[role][int(token[1])], int(token[2]))
        elif token and token[0] in "GV":
            for k in range(2):
                errors_in.settle(role, ORDERS[role][int(token[1])], k)

    for token in [token for token in plans[0] if token[0] in steps] + [""]:
        by_role(lambda role: between(role, token))
        if token and token[0] == "X":
            error(int(token[1]))
        elif token:
            steps[token[0]](int(token[1]), int(token[2]) if len(token) > 2 else 0)

    def sent(sem, count):
        part = pieces(count)
        latent_copy(part, part, sem, sem, me).wait_send()

    by_role(lambda role: sent(gather_sem, tokens_in.started[role] + errors_in.started[role]))
    pairs = 2 * groups * span * latents * 4 // (half_rows * width * 2)
    sent(sum_sem, 6 * groups + 2 * (groups - 1) + pairs)

    def finish_group(g, carry):
        pg_copy(g).wait()
        return carry

    lax.fori_loop(0, groups, finish_group, 0)
    for c in range(width // wide):
        dec_copy(c).wait()
    tok_copy.wait()


def grads_kernel(tok, pg, dec_low, dec_high, loss, enc_out, dec_out, loss_out, buf, sem):
    part = dec_low.shape[1]
    copies = [
        pltpu.make_async_copy(half, dec_out.at[:, pl.ds(i * part, part)], sem.at[i])
        for i, half in enumerate((dec_low, dec_high))
    ]
    for copy in copies:
        copy.start()
    loss_out[...] = loss[0:1, 0:1]
    width = tok.shape[1]
    tile = min(512, width)
    for i in range(width // tile):
        here = pl.ds(i * tile, tile)
        buf[here, :] = lax.dot_general(
            tok[:, here], pg[...], (((0,), (0,)), ((), ())), preferred_element_type=F32).astype(BF16)
        copies.append(pltpu.make_async_copy(buf.at[here], enc_out.at[here], sem.at[2 + i]))
        copies[-1].start()
    for copy in copies:
        copy.wait()


def fast_step(n, activations, enc_weight, enc_bias, dec_weight, dec_bias, active_mask):
    rows, width = activations.shape[1:]
    tokens, latents = active_mask.shape
    group = 4
    groups = n // group
    span = group * rows
    decoder = dec_weight[0]
    vmem = pl.BlockSpec(memory_space=pltpu.VMEM)
    anyw = pl.BlockSpec(memory_space=pl.ANY)
    shape = jax.ShapeDtypeStruct
    dma = pltpu.SemaphoreType.DMA
    def keep(x):
        return pltpu.with_memory_space_constraint(x, pltpu.HBM)

    tok, pg, dec_low, dec_high, loss = pl.pallas_call(
        functools.partial(exchange_kernel, n, group, (PLAN_END, PLAN_MID)),
        out_shape=(
            shape((n, rows, width), BF16),
            shape((n, rows, latents), BF16),
            shape((latents, width // 2), BF16),
            shape((latents, width // 2), BF16),
            shape((8, 128), F32),
        ),
        in_specs=[anyw] * 6,
        out_specs=(anyw, anyw, anyw, anyw, vmem),
        scratch_shapes=[
            pltpu.VMEM((width, latents), BF16),
            pltpu.VMEM((latents, width), BF16),
            pltpu.VMEM((n, rows, latents), jnp.int32),
            pltpu.VMEM((n, rows, width), BF16),
            pltpu.VMEM((groups, 2, span // 2, latents), F32),
            pltpu.VMEM((groups, 2, span // 2, latents), F32),
            pltpu.VMEM((n, rows, latents), BF16),
            pltpu.VMEM((n, rows, width), BF16),
            pltpu.VMEM((n, rows, width), BF16),
            pltpu.VMEM((2, groups, rows // 2, width), BF16),
            pltpu.VMEM((groups, rows, width), BF16),
            pltpu.VMEM((groups, rows, width), BF16),
            pltpu.VMEM((n, rows, width), BF16),
            pltpu.VMEM((groups, span, latents), F32),
            pltpu.VMEM((groups, span, latents), F32),
            pltpu.VMEM((width, latents), BF16),
            pltpu.VMEM((n, rows, latents), BF16),
            pltpu.VMEM((8, latents), F32),
            pltpu.VMEM((8, latents), F32),
            pltpu.VMEM((8, latents), F32),
            pltpu.VMEM((latents, 128), F32),
            pltpu.VMEM((latents, width), F32),
            pltpu.VMEM((11, 8, 128), F32),
            pltpu.VMEM((rows, width), BF16),
            pltpu.VMEM((1, latents), F32),
            pltpu.VMEM((1, width), F32),
            dma((6,)), dma((1 + groups + width // min(512, width),)),
            dma, dma, dma((n, 2)), dma((n, 2)), dma((2, groups)), dma((2, groups)), dma((2,)),
            dma((groups, 2)), dma, dma, dma((6,)), dma((11,)),
        ],
        compiler_params=pltpu.CompilerParams(
            collective_id=0, has_side_effects=True, vmem_limit_bytes=45 << 20),
    )(keep(activations[0]), enc_weight[0], keep(enc_bias[None]), decoder, keep(dec_bias),
      active_mask.reshape(n, rows, latents))
    grad_enc, grad_dec, loss = pl.pallas_call(
        grads_kernel,
        out_shape=(
            shape((width, latents), BF16),
            shape((latents, width), BF16),
            shape((1, 1), F32),
        ),
        in_specs=[vmem, vmem, anyw, anyw, vmem],
        out_specs=(anyw, anyw, vmem),
        scratch_shapes=[pltpu.VMEM((width, latents), BF16), dma((2 + width // min(512, width),))],
        compiler_params=pltpu.CompilerParams(vmem_limit_bytes=12 << 20),
    )(tok.reshape(tokens, width), pg.reshape(tokens, latents), dec_low, dec_high, loss)
    return (grad_enc[None], grad_dec[None], loss.reshape(()))


def solution(mesh):
    placed = (
        P("layer", "latent", None),
        P("layer", None, "latent"),
        P("latent"),
        P("layer", "latent", None),
        P("layer", None),
        P(None, "latent"),
    )
    n = mesh.shape["latent"]

    def per_device(activations, *others):
        rows = activations.shape[1]
        if rows == 32 and n == 16:
            return fast_step(n, activations, *others)
        return plain_step(activations, *others)

    return jax.shard_map(
        per_device,
        mesh=mesh,
        in_specs=placed,
        out_specs=(P("layer", None, "latent"), P("layer", "latent", None), P()),
        check_vma=False,
    )
```

```python
import functools

import jax
import jax.numpy as jnp
from jax import lax
from jax.experimental import pallas as pl
from jax.experimental.pallas import tpu as pltpu
from jax.sharding import PartitionSpec as P

sparsity_weight = 0.4
MESH = pl.DeviceIdType.MESH
F32 = jnp.float32
BF16 = jnp.bfloat16


PLAN_END = (
    "r00", "c10", "r01", "d00", "c11", "c20", "E01", "d01", "c30", "E00", "C01", "E10",
    "c31", "r30", "E11", "c21", "r31", "C10", "E20", "C11", "C20", "E30", "E21", "F10",
    "C30", "F20", "C21", "F11", "C00", "E31", "U20", "F30", "C31", "U10", "U11", "F21",
    "U30", "F31", "F00", "U21", "U31", "F01", "X0", "R00", "X1", "K10", "R01", "K11",
    "D00", "K20", "D01", "K21", "K31", "K30", "G0", "H0", "G1", "R30", "R31", "V1",
    "G2", "G3", "H1", "H2", "V3", "H3",
)
PLAN_MID = (
    "c00", "r10", "r11", "c20", "c01", "c30", "d10", "c31", "d11", "E01", "E00", "C01",
    "E10", "c21", "E11", "r30", "d20", "r31", "C10", "E20", "C11", "d21", "C20", "E30",
    "E21", "C30", "F00", "F20", "C21", "C00", "F30", "E31", "F21", "C31", "U20", "U30",
    "F01", "U21", "F31", "F11", "F10", "U00", "U01", "U31", "X0", "R10", "X1", "K00",
    "D10", "K20", "R11", "K21", "K01", "K30", "D11", "G0", "K31", "D21", "R30", "H0",
    "D20", "G1", "R31", "V1", "G2", "G3", "H1", "H2", "V3", "H3",
)
ORDERS = ((0, 1, 2, 3), (1, 0, 2, 3))
CORNER_UP = ({0: (1,)}, {1: (1, -1), 2: (-1,)})


def plain_step(activations, enc_weight, enc_bias, dec_weight, dec_bias, active_mask):
    local_rows = activations[0]
    encoder = enc_weight[0]
    decoder = dec_weight[0]
    token_all = lax.all_gather(local_rows, "latent", axis=0, tiled=True)
    layer_pre = jnp.dot(token_all, encoder, preferred_element_type=jnp.float32)
    dec_float = decoder.astype(jnp.float32)
    row_norm = jnp.sqrt(jnp.sum(dec_float * dec_float, axis=1) + 1e-06)
    preact, norm_sum = lax.psum((layer_pre, row_norm), "layer")
    preact = preact + enc_bias
    gating = active_mask.astype(jnp.float32)
    latent_code = preact * gating
    code_b = latent_code.astype(jnp.bfloat16)
    layer_index = lax.axis_index("layer")
    recon_share = (
        lax.psum_scatter(
            jnp.dot(code_b, decoder, preferred_element_type=jnp.float32),
            "latent",
            scatter_dimension=0,
            tiled=True,
        )
        + dec_bias[0]
    )
    error_share = recon_share - local_rows.astype(jnp.float32)
    square_part = 0.5 * jnp.sum(error_share * error_share)
    error_b = lax.all_gather(error_share.astype(jnp.bfloat16), "latent", axis=0, tiled=True)
    layer_grad = jnp.einsum("td,fd->tf", error_b, decoder, preferred_element_type=jnp.float32)
    code_grad = lax.psum(layer_grad, "layer") + sparsity_weight * norm_sum
    preact_grad = (code_grad * gating).astype(jnp.bfloat16)
    grad_enc = jnp.einsum(
        "td,tf->df", token_all, preact_grad, preferred_element_type=jnp.float32
    ).astype(jnp.bfloat16)
    code_total = jnp.sum(latent_code, axis=0)
    shrink = sparsity_weight * code_total[:, None] * dec_float / row_norm[:, None]
    grad_dec = (
        jnp.einsum("tf,td->fd", code_b, error_b, preferred_element_type=jnp.float32) + shrink
    ).astype(jnp.bfloat16)
    sparse_part = jnp.where(
        layer_index == 0, sparsity_weight * jnp.sum(latent_code * norm_sum), 0.0
    )
    loss_total = lax.psum(square_part + sparse_part, ("layer", "latent"))
    loss_value = loss_total / (active_mask.shape[0] * token_all.shape[1])
    return (grad_enc[None], grad_dec[None], loss_value)


def exchange_kernel(n, group, plans, act_hbm, enc_hbm, bias_hbm, dec_hbm, dbias_hbm, mask_hbm,
                    tok_out, pg_out, dec_low, dec_high, loss_out,
                    enc, dec, mask, tok, pre_own, pre_recv, code,
                    rs_send, rs_recv, rs_half, up_send, up_recv, err, lg_own, lg_recv, dec_t, pg,
                    norm_own, norm_recv, total, coef, acc, loss_all, act, bias, dbias,
                    load_sem, out_sem,
                    gather_sem, sum_sem, ag_r, er_r, rs_r, rs_hr, up_r,
                    pair_r, nm_s, nm_r, ls_s, ls_r):
    me = lax.axis_index("latent")
    layer = lax.axis_index("layer")
    other = 1 - layer
    rows, width = act.shape
    latents = mask.shape[2]
    tokens = n * rows
    span = group * rows
    groups = n // group
    mine = me // group
    spot = lax.rem(me, group)
    low = mine < groups // 2
    at_end = (mine == 0) | (mine == groups - 1)
    toward = jnp.where(low, 1, -1)

    def plane(q):
        return jnp.where(low, q, groups - 1 - q)

    def place(step):
        return plane(jnp.where(at_end, ORDERS[0][step], ORDERS[1][step]))

    side_x = spot ^ 1
    side_y = spot ^ 2
    corner = spot ^ 3
    sides = (side_x, side_y)
    half_rows = rows // 2
    half_span = span // 2

    def half(k):
        return pl.ds(k * half_rows, half_rows)

    def block_of(g):
        return pl.ds(g * group, group)

    loads = [
        pltpu.make_async_copy(hbm, vmem, load_sem.at[i])
        for i, (hbm, vmem) in enumerate((
            (act_hbm, act), (dec_hbm, dec), (enc_hbm, enc), (mask_hbm, mask),
            (bias_hbm, bias), (dbias_hbm, dbias)))
    ]
    for load in loads:
        load.start()

    barrier = pltpu.get_barrier_semaphore()
    others = [lax.rem(mine + k, groups) * group + spot for k in range(1, groups)]
    partners = [mine * group + side_x, mine * group + side_y] + others
    for partner in partners:
        pl.semaphore_signal(barrier, inc=1, device_id={"latent": partner}, device_id_type=MESH)
    pl.semaphore_signal(barrier, inc=1, device_id={"layer": other}, device_id_type=MESH)
    pl.semaphore_wait(barrier, len(partners) + 1)

    def latent_copy(src, dst, send, recv, target):
        return pltpu.make_async_remote_copy(
            src_ref=src, dst_ref=dst, send_sem=send, recv_sem=recv,
            device_id={"latent": target}, device_id_type=MESH)

    def layer_copy(src, dst, send, recv):
        return pltpu.make_async_remote_copy(
            src_ref=src, dst_ref=dst, send_sem=send, recv_sem=recv,
            device_id={"layer": other}, device_id_type=MESH)

    class Gather:
        def __init__(self, buf, first, recv_sem, far):
            self.buf, self.first, self.recv_sem, self.far = buf, first, recv_sem, far
            self.started = [0, 0]
            self.seen = (set(), set())

        def piece(self, q, where, k):
            return self.buf.at[plane(q) * group + where, half(k)]

        def wait(self, role, q, where, k, key):
            if (key, q, k) in self.seen[role]:
                return
            self.seen[role].add((key, q, k))
            part = self.piece(q, where, k)
            latent_copy(
                part, part, gather_sem,
                self.recv_sem.at[plane(q) * group + where, k], me).wait_recv()

        def send(self, role, q, where, k, target, own=False):
            part = self.piece(q, where, k)
            latent_copy(
                self.first.at[half(k)] if own else part, part, gather_sem,
                self.recv_sem.at[plane(q) * group + where, k], target()).start()
            self.started[role] += 1

        def along(self, role, q, where, k, shift, own=False):
            self.send(role, q, where, k, lambda: me + shift * toward * group, own)

        def across(self, role, q, k, own=False):
            for to in sides:
                self.send(role, q, spot, k, lambda to=to: mine * group + to, own)

        def run(self, role, event, q, k):
            if event == "o":
                self.across(role, q, k, own=True)
                for shift in ((1, groups - 1) if self.far[k] else (1,), (1, -1))[role]:
                    self.along(role, q, spot, k, shift, own=True)
            elif event == "c":
                self.wait(role, q, spot, k, "s")
                if role == 1 and not (q == groups - 1 and self.far[k]):
                    self.along(role, q, spot, k, 1 if q == 0 else -1)
                self.across(role, q, k)
            elif event == "r":
                self.wait(role, q, sides[k], k, "xy"[k])
                self.send(role, q, sides[k], k, lambda: mine * group + sides[1 - k])
            else:
                self.wait(role, q, corner, k, "d")
                for shift in CORNER_UP[role].get(q, ()):
                    self.along(role, q, corner, k, shift)

        def settle(self, role, q, k):
            if q != role:
                self.wait(role, q, spot, k, "s")
            self.wait(role, q, side_x, k, "x")
            self.wait(role, q, side_y, k, "y")
            self.wait(role, q, corner, k, "d")

    tokens_in = Gather(tok, act, ag_r, (False, False))
    errors_in = Gather(err, err.at[me], er_r, (False, True))

    def by_role(do):
        @pl.when(at_end)
        def _():
            do(0)

        @pl.when(jnp.logical_not(at_end))
        def _():
            do(1)

    def pre_copy(g, k):
        return layer_copy(pre_own.at[g, k], pre_recv.at[g, k], sum_sem, pair_r.at[g, k])

    def lg_copy(g):
        return layer_copy(lg_own.at[g], lg_recv.at[g], sum_sem, pair_r.at[g, 0])

    def corner_copy(g, k):
        return latent_copy(
            rs_send.at[g * group + corner, half(k)], rs_half.at[k, g],
            sum_sem, rs_hr.at[k, g], mine * group + sides[1 - k])

    def side_copy(g, i, k):
        return latent_copy(
            rs_send.at[g * group + sides[i], half(k)], rs_recv.at[g * group + spot, half(k)],
            sum_sem, rs_r.at[k, g], mine * group + sides[i])

    def pieces(count):
        return acc.at[pl.ds(0, count * half_rows // 2)]

    def side_arrived(g, k):
        part = pieces(2)
        latent_copy(part, part, sum_sem, rs_r.at[k, g], me).wait_recv()

    def up_copy(g, k):
        return latent_copy(
            up_send.at[g, half(k)], up_recv.at[mine, half(k)],
            sum_sem, up_r.at[k], g * group + spot)

    def up_arrived(k):
        part = pieces(groups - 1)
        latent_copy(part, part, sum_sem, up_r.at[k], me).wait_recv()

    tile = min(512, latents)
    wide = min(512, width)
    lanes = 128

    def norm_block(block, carry):
        at = pl.multiple_of(block * lanes, lanes)
        piece = dec[pl.ds(at, lanes), :].astype(F32)
        dec_t[:, pl.ds(at, lanes)] = dec[pl.ds(at, lanes), :].T
        sums = jnp.sum(piece * piece, axis=1, keepdims=True)
        norm = jnp.sqrt(sums + 1e-06)
        norm_own[:, pl.ds(at, lanes)] = jnp.broadcast_to(norm, (lanes, lanes)).T[0:8, :]
        return carry

    norm_copy = layer_copy(norm_own, norm_recv, nm_s, nm_r)

    def encode(step, k):
        g = place(step)
        left = tok[block_of(g), half(k)].reshape(half_span, width)
        for c in range(latents // tile):
            cols = pl.ds(c * tile, tile)
            pre_own[g, k, :, cols] = jnp.dot(left, enc[:, cols], preferred_element_type=F32)
        pre_copy(g, k).start()

    def decode(step, k):
        g = place(step)
        pre_copy(g, k).wait_recv()
        for c in range(latents // tile):
            cols = pl.ds(c * tile, tile)
            gating = mask[block_of(g), half(k), cols].reshape(half_span, tile).astype(F32)
            preact = pre_own[g, k, :, cols] + pre_recv[g, k, :, cols] + bias[0:1, cols]
            latent = preact * gating
            total[0:1, cols] += jnp.sum(latent, axis=0, keepdims=True)
            code[block_of(g), half(k), cols] = latent.astype(BF16).reshape(group, half_rows, tile)
        left = code[block_of(g), half(k)].reshape(half_span, latents)
        for c in range(width // wide):
            cols = pl.ds(c * wide, wide)
            part = jnp.dot(left, dec[:, cols], preferred_element_type=F32).astype(BF16)
            rs_send[block_of(g), half(k), cols] = part.reshape(group, half_rows, wide)
        corner_copy(g, k).start()
        side_copy(g, 1 - k, k).start()

    def fold(q, k):
        g = plane(q)
        part = rs_half.at[k, g]
        latent_copy(part, part, sum_sem, rs_hr.at[k, g], me).wait_recv()
        at = (g * group + sides[k], half(k))
        rs_send[at] = (rs_send[at].astype(F32) + rs_half[k, g].astype(F32)).astype(BF16)
        side_copy(g, k, k).start()

    def plane_sum(g, k, cols):
        part = rs_send[g * group + spot, half(k), cols].astype(F32)
        for source in sides:
            part = part + rs_recv[g * group + source, half(k), cols].astype(F32)
        return part

    def climb(q, k):
        g = plane(q)
        side_arrived(g, k)
        for c in range(width // wide):
            cols = pl.ds(c * wide, wide)
            up_send[g, half(k), cols] = plane_sum(g, k, cols).astype(BF16)
        up_copy(g, k).start()

    squares = []

    def error(k):
        side_arrived(mine, k)
        planes = [lax.rem(mine + j, groups) for j in range(1, groups)]
        up_arrived(k)
        for c in range(width // wide):
            cols = pl.ds(c * wide, wide)
            recon = plane_sum(mine, k, cols)
            for g in planes:
                recon = recon + up_recv[g, half(k), cols].astype(F32)
            gap = recon + dbias[0:1, cols] - act[half(k), cols].astype(F32)
            squares.append(jnp.sum(gap * gap))
            err[me, half(k), cols] = gap.astype(BF16)
        by_role(lambda role: errors_in.run(role, "o", role, k))
        if len(squares) == 2 * (width // wide):
            settle_sums()

    def loss_copy(index, source, slot, target):
        return latent_copy(
            loss_all.at[source], loss_all.at[slot], ls_s.at[index], ls_r.at[slot], target)

    def loss_z(j):
        return loss_copy(j + 1, 4, 5 + mine, others[j - 1])

    def loss_pair():
        return layer_copy(loss_all.at[9], loss_all.at[10], ls_s.at[5], ls_r.at[10])

    def settle_sums():
        tok_copy.start()
        norm_copy.wait()
        norm_sum = norm_own[0:1, :] + norm_recv[0:1, :]
        sparse = sparsity_weight * jnp.sum(total[0:1, :] * norm_sum)
        ratio = sparsity_weight * total[0:1, :] / norm_own[0:1, :]
        coef[...] = jnp.broadcast_to(ratio, (lanes, latents)).T
        norm_recv[...] = jnp.broadcast_to(sparsity_weight * norm_sum, norm_recv.shape)
        partial = 0.5 * sum(squares) + jnp.where(layer == 0, sparse, 0.0)
        loss_all[0] = jnp.broadcast_to(partial, loss_all.shape[1:])
        loss_copy(0, 0, 1, partners[0]).start()

    def loss_step(step):
        if step == 0:
            loss_copy(0, 0, 1, partners[0]).wait()
            loss_all[2] = loss_all[0] + loss_all[1]
            loss_copy(1, 2, 3, partners[1]).start()
        elif step == 1:
            loss_copy(1, 2, 3, partners[1]).wait()
            loss_all[4] = loss_all[2] + loss_all[3]
            loss_all[5 + mine] = loss_all[4]
            for j in range(1, groups):
                loss_z(j).start()
        elif step == 2:
            for j in range(1, groups):
                latent_copy(
                    loss_all.at[4], loss_all.at[5 + lax.rem(mine + j, groups)],
                    ls_s.at[j + 1], ls_r.at[5 + lax.rem(mine + j, groups)], me).wait_recv()
                loss_z(j).wait_send()
            loss_all[9] = loss_all[5] + loss_all[6] + loss_all[7] + loss_all[8]
            loss_pair().start()
        else:
            loss_pair().wait()
            loss_out[...] = (loss_all[9] + loss_all[10]) / (tokens * width)

    def grad(step, k):
        g = place(step)
        left = err[block_of(g)].reshape(span, width)
        for c in range(latents // tile):
            cols = pl.ds(c * tile, tile)
            lg_own[g, :, cols] = jnp.dot(left, dec_t[:, cols], preferred_element_type=F32)
        lg_copy(g).start()
        loss_step(step)

    def gate(step, k):
        g = place(step)
        lg_copy(g).wait_recv()
        for c in range(latents // tile):
            cols = pl.ds(c * tile, tile)
            gating = mask[block_of(g), :, cols].reshape(span, tile).astype(F32)
            code_grad = lg_own[g, :, cols] + lg_recv[g, :, cols] + norm_recv[0:1, cols]
            pg[block_of(g), :, cols] = (code_grad * gating).astype(BF16).reshape(group, rows, tile)
        pg_copy(g).start()

    def pg_copy(g):
        return pltpu.make_async_copy(pg.at[block_of(g)], pg_out.at[block_of(g)], out_sem.at[1 + g])

    def dec_copy(c):
        cols = pl.ds(c * wide, wide)
        part = width // 2
        out = (dec_low, dec_high)[c * wide // part]
        return pltpu.make_async_copy(
            dec.at[:, cols], out.at[:, pl.ds(c * wide % part, wide)], out_sem.at[1 + groups + c])

    def outer(step, k):
        blocks = [block_of(place(step - 1)), block_of(place(step))]
        left = jnp.concatenate([code[b].reshape(span, latents) for b in blocks], axis=0)
        right = jnp.concatenate([err[b].reshape(span, width) for b in blocks], axis=0)
        for c in range(width // wide):
            cols = pl.ds(c * wide, wide)
            part = lax.dot_general(
                left, right[:, c * wide:(c + 1) * wide], (((0,), (0,)), ((), ())),
                preferred_element_type=F32)
            if step == 1:
                acc[:, cols] = part + coef[:, 0:1] * dec[:, cols].astype(F32)
            elif step < groups - 1:
                acc[:, cols] += part
            else:
                dec[:, cols] = (acc[:, cols] + part).astype(BF16)
                dec_copy(c).start()

    tok_copy = pltpu.make_async_copy(tok, tok_out, out_sem.at[0])

    def open_tokens(k):
        by_role(lambda role: tokens_in.run(role, "o", role, k))

    loads[0].wait()
    for k in range(2):
        open_tokens(k)
    tok[me] = act[...]
    loads[1].wait()
    lax.fori_loop(0, latents // lanes, norm_block, 0)
    norm_copy.start()
    total[...] = jnp.zeros_like(total)
    for load in loads[2:]:
        load.wait()

    steps = {"E": encode, "C": decode, "X": error, "G": grad, "V": outer, "H": gate}
    taken = [0, 0]

    def between(role, token):
        plan = plans[role]
        while taken[role] < len(plan) and plan[taken[role]][0] not in steps:
            event = plan[taken[role]]
            q, k = int(event[1]), int(event[2])
            if event[0] == "F":
                fold(q, k)
            elif event[0] == "U":
                climb(q, k)
            elif event[0] in "crd":
                tokens_in.run(role, event[0], q, k)
            else:
                errors_in.run(role, event[0].lower().replace("k", "c"), q, k)
            taken[role] += 1
        taken[role] += 1
        if token and token[0] == "E":
            tokens_in.settle(role, ORDERS[role][int(token[1])], int(token[2]))
        elif token and token[0] in "GV":
            for k in range(2):
                errors_in.settle(role, ORDERS[role][int(token[1])], k)

    for token in [token for token in plans[0] if token[0] in steps] + [""]:
        by_role(lambda role: between(role, token))
        if token and token[0] == "X":
            error(int(token[1]))
        elif token:
            steps[token[0]](int(token[1]), int(token[2]) if len(token) > 2 else 0)

    def sent(sem, count):
        part = pieces(count)
        latent_copy(part, part, sem, sem, me).wait_send()

    by_role(lambda role: sent(gather_sem, tokens_in.started[role] + errors_in.started[role]))
    pairs = 2 * groups * span * latents * 4 // (half_rows * width * 2)
    sent(sum_sem, 6 * groups + 2 * (groups - 1) + pairs)

    def finish_group(g, carry):
        pg_copy(g).wait()
        return carry

    lax.fori_loop(0, groups, finish_group, 0)
    for c in range(width // wide):
        dec_copy(c).wait()
    tok_copy.wait()


def grads_kernel(tok, pg, dec_low, dec_high, loss, enc_out, dec_out, loss_out, buf, sem):
    part = dec_low.shape[1]
    copies = [
        pltpu.make_async_copy(half, dec_out.at[:, pl.ds(i * part, part)], sem.at[i])
        for i, half in enumerate((dec_low, dec_high))
    ]
    for copy in copies:
        copy.start()
    loss_out[...] = loss[0:1, 0:1]
    width = tok.shape[1]
    tile = min(512, width)
    for i in range(width // tile):
        here = pl.ds(i * tile, tile)
        buf[here, :] = lax.dot_general(
            tok[:, here], pg[...], (((0,), (0,)), ((), ())), preferred_element_type=F32).astype(BF16)
        copies.append(pltpu.make_async_copy(buf.at[here], enc_out.at[here], sem.at[2 + i]))
        copies[-1].start()
    for copy in copies:
        copy.wait()


def fast_step(n, activations, enc_weight, enc_bias, dec_weight, dec_bias, active_mask):
    rows, width = activations.shape[1:]
    tokens, latents = active_mask.shape
    group = 4
    groups = n // group
    span = group * rows
    decoder = dec_weight[0]
    vmem = pl.BlockSpec(memory_space=pltpu.VMEM)
    anyw = pl.BlockSpec(memory_space=pl.ANY)
    shape = jax.ShapeDtypeStruct
    dma = pltpu.SemaphoreType.DMA
    def keep(x):
        return pltpu.with_memory_space_constraint(x, pltpu.HBM)

    tok, pg, dec_low, dec_high, loss = pl.pallas_call(
        functools.partial(exchange_kernel, n, group, (PLAN_END, PLAN_MID)),
        out_shape=(
            shape((n, rows, width), BF16),
            shape((n, rows, latents), BF16),
            shape((latents, width // 2), BF16),
            shape((latents, width // 2), BF16),
            shape((8, 128), F32),
        ),
        in_specs=[anyw] * 6,
        out_specs=(anyw, anyw, anyw, anyw, vmem),
        scratch_shapes=[
            pltpu.VMEM((width, latents), BF16),
            pltpu.VMEM((latents, width), BF16),
            pltpu.VMEM((n, rows, latents), jnp.int32),
            pltpu.VMEM((n, rows, width), BF16),
            pltpu.VMEM((groups, 2, span // 2, latents), F32),
            pltpu.VMEM((groups, 2, span // 2, latents), F32),
            pltpu.VMEM((n, rows, latents), BF16),
            pltpu.VMEM((n, rows, width), BF16),
            pltpu.VMEM((n, rows, width), BF16),
            pltpu.VMEM((2, groups, rows // 2, width), BF16),
            pltpu.VMEM((groups, rows, width), BF16),
            pltpu.VMEM((groups, rows, width), BF16),
            pltpu.VMEM((n, rows, width), BF16),
            pltpu.VMEM((groups, span, latents), F32),
            pltpu.VMEM((groups, span, latents), F32),
            pltpu.VMEM((width, latents), BF16),
            pltpu.VMEM((n, rows, latents), BF16),
            pltpu.VMEM((8, latents), F32),
            pltpu.VMEM((8, latents), F32),
            pltpu.VMEM((8, latents), F32),
            pltpu.VMEM((latents, 128), F32),
            pltpu.VMEM((latents, width), F32),
            pltpu.VMEM((11, 8, 128), F32),
            pltpu.VMEM((rows, width), BF16),
            pltpu.VMEM((1, latents), F32),
            pltpu.VMEM((1, width), F32),
            dma((6,)), dma((1 + groups + width // min(512, width),)),
            dma, dma, dma((n, 2)), dma((n, 2)), dma((2, groups)), dma((2, groups)), dma((2,)),
            dma((groups, 2)), dma, dma, dma((6,)), dma((11,)),
        ],
        compiler_params=pltpu.CompilerParams(
            collective_id=0, has_side_effects=True, vmem_limit_bytes=45 << 20),
    )(keep(activations[0]), enc_weight[0], keep(enc_bias[None]), decoder, keep(dec_bias),
      active_mask.reshape(n, rows, latents))
    grad_enc, grad_dec, loss = pl.pallas_call(
        grads_kernel,
        out_shape=(
            shape((width, latents), BF16),
            shape((latents, width), BF16),
            shape((1, 1), F32),
        ),
        in_specs=[vmem, vmem, anyw, anyw, vmem],
        out_specs=(anyw, anyw, vmem),
        scratch_shapes=[pltpu.VMEM((width, latents), BF16), dma((2 + width // min(512, width),))],
        compiler_params=pltpu.CompilerParams(vmem_limit_bytes=12 << 20),
    )(tok.reshape(tokens, width), pg.reshape(tokens, latents), dec_low, dec_high, loss)
    return (grad_enc[None], grad_dec[None], loss.reshape(()))


def solution(mesh):
    placed = (
        P("layer", "latent", None),
        P("layer", None, "latent"),
        P("latent"),
        P("layer", "latent", None),
        P("layer", None),
        P(None, "latent"),
    )
    n = mesh.shape["latent"]

    def per_device(activations, *others):
        rows = activations.shape[1]
        if rows == 32 and n == 16:
            return fast_step(n, activations, *others)
        return plain_step(activations, *others)

    return jax.shard_map(
        per_device,
        mesh=mesh,
        in_specs=placed,
        out_specs=(P("layer", None, "latent"), P("layer", "latent", None), P()),
        check_vma=False,
    )
```
